256 devices in a mesh: pop: 64 (over y, x, z_lo), tp: 4 (over z_hi, core).
Axes of the slice: x: 4, y: 4, z: 8 (z_hi: 2, z_lo: 4; z = z_hi * 4 + z_lo), core: 2. Of those that a mesh axis runs over, the one named last changes fastest.
Arguments:
- tokens: bfloat16 [64, 256, 4096], P('pop', None, 'tp'), may hold values from -6 to 6
- receptance: bfloat16 [64, 256, 4096], P('pop', None, 'tp'), may hold values from -6 to 6
- keys: bfloat16 [64, 256, 4096], P('pop', None, 'tp'), may hold values from -0.29882812 to 0.29882812
- log_decay: bfloat16 [64, 256, 4096], P('pop', None, 'tp'), may hold values from -1 to 0
- value_weight: bfloat16 [4096, 4096], P('pop', 'tp'), may hold values from -0.09375 to 0.09375
- noise_in: bfloat16 [64, 4096], P('pop'), may hold values from -6 to 6
- noise_out: bfloat16 [64, 4096], P('pop', 'tp'), may hold values from -6 to 6
- utilities: float32 [64], P('pop'), may hold values from -0.5 to 0.5, as said below
- live_length: int32 [64], P('pop'), may hold values from 1 to 256, as said below
Outputs:
- wkv_out: bfloat16 [64, 256, 4096], P('pop', None, 'tp')
- update: float32 [4096, 4096], P('pop', 'tp')
The draws below stay inside these ranges and needn't reach their ends.
Inputs may be any that keep to these rules, and one draw needn't show every extreme that they name: `utilities`: centered ranks: the values k / 63 - 0.5, each taken once. tokens at positions from live_length on are masked.
All inputs are finite; a program needn't handle non-finite values.
Results may differ from the reference program's by a relative error of at most 0.0049.
Values may be sent and summed in bfloat16 or wider, within the bound.
No kernel may reach another device: no remote copies, remote signals or barrier semaphores. Data moves between devices by JAX's collectives and lax.ppermute only.
A program may use at most 128 MiB of HBM per device.

```python
import math
import jax
import jax.numpy as jnp
from jax import lax

D = 4096
HEAD = 64
HEADS = 64
MEMBERS = 64
EPISODE_SYMBOLS = 256


def draw_log_decay(key, part):
    keys_list = jax.random.split(key, 5)
    channel = jax.random.uniform(keys_list[0], (D,), minval=math.log(0.002), maxval=math.log(0.06))
    member = jax.random.uniform(keys_list[1], (MEMBERS, 1, 1), minval=math.log(0.5), maxval=math.log(2.0))
    rough = jax.random.uniform(keys_list[2], (MEMBERS, EPISODE_SYMBOLS, D), minval=0.5, maxval=1.5)
    descent_multiplier = jnp.exp(channel)[None, None, :] * jnp.exp(member) * rough
    sequence_indices = jax.random.randint(keys_list[3], (MEMBERS, 3), 0, EPISODE_SYMBOLS)
    window_extent = jnp.any(jnp.arange(EPISODE_SYMBOLS)[None, :, None] == sequence_indices[:, None, :], axis=-1)
    perturb_magnitude = jax.random.uniform(keys_list[4], (MEMBERS, EPISODE_SYMBOLS, 1), minval=0.2, maxval=0.7)
    descent_multiplier = descent_multiplier + jnp.where(window_extent[:, :, None], perturb_magnitude, 0.0)
    return (-descent_multiplier).astype(jnp.bfloat16)


def draw_utilities(key, part):
    order = jax.random.permutation(key, MEMBERS)
    return order.astype(jnp.float32) / (MEMBERS - 1) - 0.5


def draw_live_length(key, part):
    keys_list = jax.random.split(key, 3)
    lengths = jax.random.randint(keys_list[0], (MEMBERS,), 1, EPISODE_SYMBOLS + 1)
    first = jax.random.randint(keys_list[1], (), 0, MEMBERS)
    second = (first + jax.random.randint(keys_list[2], (), 1, MEMBERS)) % MEMBERS
    lengths = lengths.at[first].set(EPISODE_SYMBOLS)
    lengths = lengths.at[second].set(1)
    return lengths.astype(jnp.int32)


def block_scale(stream_key, extent, cuts, smallest, high):
    def one(position, shards_of):
        steps = jax.random.uniform(jax.random.fold_in(jax.random.fold_in(stream_key, 6), position), (shards_of,), jnp.float32, smallest / len(cuts), high / len(cuts))
        return jnp.repeat(jnp.exp(steps), extent[position] // shards_of).reshape((-1,) + (1,) * (len(extent) - position - 1))

    level = one(*cuts[0])
    for cut in cuts[1:]:
        level = level * one(*cut)
    return level


def bell_draw(rng, extent, scale, most, cuts=(), held_as=jnp.bfloat16):
    array = jax.random.normal(rng, extent, jnp.float32) * scale
    if len(cuts) > 0:
        array = block_scale(rng, extent, cuts, -0.22, 0.18) * array
    return jnp.clip(array, min=-most, max=most).astype(held_as)


def setup_inputs(seed: int = 0) -> dict:
    seeds = jax.random.split(jax.random.key(seed), 10)
    return {
        "tokens": bell_draw(seeds[0], (MEMBERS, EPISODE_SYMBOLS, D), 1.0, 6.0, ((0, 64), (2, 4))),
        "receptance": bell_draw(seeds[1], (MEMBERS, EPISODE_SYMBOLS, D), 1.0, 6.0, ((0, 64), (2, 4))),
        "keys": bell_draw(seeds[2], (MEMBERS, EPISODE_SYMBOLS, D), 0.05, 0.29882812, ((0, 64), (2, 4))),
        "log_decay": draw_log_decay(jax.random.fold_in(seeds[9], 71), 0),
        "value_weight": bell_draw(seeds[4], (D, D), D ** -0.5, 0.09375, ((0, 64), (1, 4))),
        "noise_in": bell_draw(seeds[5], (MEMBERS, D), 1.0, 6.0, ((0, 64),)),
        "noise_out": bell_draw(seeds[6], (MEMBERS, D), 1.0, 6.0, ((0, 64), (1, 4))),
        "utilities": draw_utilities(jax.random.fold_in(seeds[9], 71), 0),
        "live_length": draw_live_length(jax.random.fold_in(seeds[9], 71), 0),
    }


HIGHEST = lax.Precision.HIGHEST
SIGMA = 0.5

def wkv_block(weighted_key_value_state, recept, masked_keys, masked_decay, value_items):
    cum_log = jnp.cumsum(masked_decay, axis=0)
    span_len = recept.shape[0]
    lower_mask = jnp.arange(span_len)[:, None] >= jnp.arange(span_len)[None, :]
    grown_recept = recept * jnp.exp(cum_log)
    shrunk_keys = masked_keys * jnp.exp(-cum_log)
    scores = jnp.where(lower_mask, jnp.dot(grown_recept, shrunk_keys.T, precision=HIGHEST), 0.0)
    block_out = jnp.dot(grown_recept, weighted_key_value_state, precision=HIGHEST) + jnp.dot(scores, value_items, precision=HIGHEST)
    final_log = cum_log[-1]
    carried = (masked_keys * jnp.exp(final_log[None, :] - cum_log)).T
    weighted_key_value_state = jnp.exp(final_log)[:, None] * weighted_key_value_state + jnp.dot(carried, value_items, precision=HIGHEST)
    return (weighted_key_value_state, block_out)

def wkv_sequence(recept, masked_keys, masked_decay, value_items):
    length, head_size = recept.shape
    block_len = min(32, length)
    weighted_key_value_state = jnp.zeros((head_size, head_size), jnp.float32)
    pieces = []
    for offset in range(0, length, block_len):
        weighted_key_value_state, block_out = wkv_block(weighted_key_value_state, recept[offset:offset + block_len], masked_keys[offset:offset + block_len], masked_decay[offset:offset + block_len], value_items[offset:offset + block_len])
        pieces.append(block_out)
    return jnp.concatenate(pieces, 0)

def to_heads(array_in):
    return array_in.reshape(EPISODE_SYMBOLS, HEADS, HEAD).transpose(1, 0, 2)

def per_member(operands):
    recept, key_rows, decay_rows, value_rows, live_row = operands
    emitted_vector = jax.vmap(wkv_sequence)(to_heads(recept.astype(jnp.float32)), to_heads(key_rows.astype(jnp.float32) * live_row[:, None]), to_heads(decay_rows.astype(jnp.float32) * live_row[:, None]), to_heads(value_rows.astype(jnp.float32)))
    return (emitted_vector.transpose(1, 0, 2).reshape(EPISODE_SYMBOLS, D) * live_row[:, None]).astype(jnp.bfloat16)

def reference(tokens, receptance, keys, log_decay, value_weight, noise_in, noise_out, utilities, live_length):
    live_mask = (jnp.arange(EPISODE_SYMBOLS)[None, :] < live_length[:, None]).astype(jnp.float32)
    base_value = jnp.dot(tokens.reshape(MEMBERS * EPISODE_SYMBOLS, D), value_weight, preferred_element_type=jnp.float32).reshape(MEMBERS, EPISODE_SYMBOLS, D)
    projected = jnp.einsum('mtd,md->mt', tokens.astype(jnp.float32), noise_in.astype(jnp.float32), precision=HIGHEST)
    values = (base_value + SIGMA / math.sqrt(D) * projected[:, :, None] * noise_out.astype(jnp.float32)[:, None, :]).astype(jnp.bfloat16)
    wkv_out = lax.map(per_member, (receptance, keys, log_decay, values, live_mask))
    weighted = noise_in.astype(jnp.float32) * (utilities / math.sqrt(MEMBERS))[:, None]
    update = lax.dot_general(weighted, noise_out.astype(jnp.float32), (((0,), (0,)), ((), ())), precision=HIGHEST)
    return (wkv_out, update)
```

```python
import functools
import math

import jax
import jax.numpy as jnp
from jax import lax
from jax.experimental import pallas as pl
from jax.experimental.pallas import tpu as pltpu
from jax.sharding import PartitionSpec as P

HEAD = 64
SIGMA = 0.5
HIGHEST = lax.Precision.HIGHEST
F32 = jnp.float32
BF16 = jnp.bfloat16

SIDE = 4
STRIDE = {"y": 16, "x": 4, "z": 1}
SPAN = 64
LANES = 128

VMEM = pl.BlockSpec(memory_space=pltpu.VMEM)
SMEM = pl.BlockSpec(memory_space=pltpu.SMEM)


def fetch(array, axis, step):
    stride = STRIDE[axis]
    pairs = []
    for me in range(SIDE**3):
        at = (me // stride) % SIDE
        pairs.append((me + ((at + step) % SIDE - at) * stride, me))
    return lax.ppermute(array, "pop", pairs)


def swap(array, bit):
    return lax.ppermute(array, "tp", [(i, i ^ bit) for i in range(4)])


def join_kernel(at_ref, p0, p1, p2, p3, left_ref, right_ref):
    rows = p0.shape[0]
    half = left_ref.shape[1]
    for step, part in enumerate((p0, p1, p2, p3)):
        place = pl.ds(pl.multiple_of(lax.rem(at_ref[0] + step, SIDE) * rows, rows), rows)
        left_ref[place, :] = part[:, :half]
        right_ref[place, :] = part[:, half:]


def token_kernel(at_ref, t0, t1, t2, t3, noise_ref, tokens_ref, projected_ref):
    total = None
    for bits, part in enumerate((t0, t1, t2, t3)):
        place = jnp.bitwise_xor(at_ref[0], bits)
        block = part[...]
        tokens_ref[place] = block
        noise = jnp.broadcast_to(noise_ref[place], (8, block.shape[1]))
        term = lax.dot_general(
            block, noise, (((1,), (1,)), ((), ())), preferred_element_type=F32
        )
        total = term if total is None else total + term
    projected_ref[...] = total


def score_kernel(live_ref, recept_ref, keys_ref, decay_ref, high_ref, low_ref):
    length = recept_ref.shape[0]
    live = live_ref[0]
    row = lax.broadcasted_iota(jnp.int32, (length, LANES), 0)
    alive = row < live
    decay = jnp.where(alive, decay_ref[...], jnp.zeros((), BF16))
    keys = jnp.where(alive, keys_ref[...].astype(F32), 0.0)
    lower = (
        lax.broadcasted_iota(jnp.int32, (length, length), 0)
        >= lax.broadcasted_iota(jnp.int32, (length, length), 1)
    ).astype(F32).astype(BF16)
    summed = jnp.dot(lower, decay, preferred_element_type=F32)
    lane = lax.broadcasted_iota(jnp.int32, (SPAN, LANES), 1)
    for chunk in range(length // SPAN):
        first, last = chunk * SPAN, (chunk + 1) * SPAN
        base = summed[first - 1 : first] if chunk else jnp.zeros((1, LANES), F32)
        grown = recept_ref[first:last].astype(F32) * jnp.exp(summed[first:last] - base)
        shrunk = keys[:last] * jnp.exp(base - summed[:last])
        both = jnp.concatenate(
            [jnp.where(lane < HEAD, grown, 0.0), jnp.where(lane < HEAD, 0.0, grown)], 0
        )
        scores = lax.dot_general(
            both, shrunk, (((1,), (1,)), ((), ())), precision=HIGHEST, preferred_element_type=F32
        )
        for head in range(2):
            mine = scores[head * SPAN : (head + 1) * SPAN]
            here = lax.broadcasted_iota(jnp.int32, (SPAN, last), 0) + first
            there = lax.broadcasted_iota(jnp.int32, (SPAN, last), 1)
            mine = jnp.where((here >= there) & (here < live), mine, 0.0)
            high = mine.astype(BF16)
            low = (mine - high.astype(F32)).astype(BF16)
            high_ref[head, first:last, :last] = high
            low_ref[head, first:last, :last] = low
            if last < length:
                rest = jnp.zeros((SPAN, length - last), BF16)
                high_ref[head, first:last, last:] = rest
                low_ref[head, first:last, last:] = rest


def readout_kernel(count, at_ref, *refs):
    pieces = refs[: 2 * count]
    tokens_ref, projected_ref, noise_ref, high_ref, low_ref, out_ref = refs[2 * count :]
    y, x = at_ref[0], at_ref[1]
    depth, half = pieces[0].shape
    projected = projected_ref[...][:, :1]
    lane = lax.broadcasted_iota(jnp.int32, (out_ref.shape[0], LANES), 1)
    for side in range(2):
        total = None
        for dy in range(SIDE):
            for dx in range(SIDE):
                block = tokens_ref[
                    lax.rem(y + dy, SIDE),
                    :,
                    pl.ds(pl.multiple_of(lax.rem(x + dx, SIDE) * depth, depth), depth),
                ]
                term = jnp.dot(
                    block,
                    pieces[side * count + dy * SIDE + dx][...],
                    preferred_element_type=F32,
                )
                total = term if total is None else total + term
        noise = noise_ref[:, side * half : (side + 1) * half].astype(F32)
        values = (total + (SIGMA / math.sqrt(SIDE**3 * 64)) * projected * noise).astype(BF16)
        for pair in range(half // LANES):
            mine = values[:, pair * LANES : (pair + 1) * LANES]
            head = side * (half // HEAD) + 2 * pair
            outs = [
                jnp.dot(high_ref[head + i], mine, preferred_element_type=F32)
                + jnp.dot(low_ref[head + i], mine, preferred_element_type=F32)
                for i in range(2)
            ]
            start = side * half + pair * LANES
            out_ref[:, start : start + LANES] = jnp.where(lane < HEAD, *outs).astype(BF16)


def params(mib):
    return pltpu.CompilerParams(vmem_limit_bytes=mib << 20)


def body(
    tokens, receptance, keys, log_decay, value_weight, noise_in, noise_out, utilities, live_length
):
    _, length, width = receptance.shape
    full = noise_in.shape[1]
    pop = lax.axis_index("pop")
    tp = lax.axis_index("tp")
    y, x, z = pop // 16, (pop // 4) % SIDE, pop % SIDE
    tokens, receptance, keys, log_decay = (
        a.reshape(length, width) for a in (tokens, receptance, keys, log_decay)
    )
    rows = value_weight.shape[0]
    half = width // 2

    near = [value_weight] + [fetch(value_weight, "z", s) for s in (1, 2, 3)]
    left, right = pl.pallas_call(
        join_kernel,
        out_shape=[jax.ShapeDtypeStruct((SIDE * rows, half), BF16)] * 2,
        in_specs=[SMEM] + [VMEM] * 4,
        out_specs=[VMEM] * 2,
        name="join_rows",
    )(z.reshape(1), *near)

    (left, right), tokens = lax.optimization_barrier(((left, right), tokens))
    twin = swap(tokens, 2)
    mate = swap(tokens, 1)
    both = swap(twin, 1)

    lefts = {(0, 0): left}
    rights = {(0, 0): right}
    for s in (1, 3, 2):
        lefts[0, s] = fetch(left, "x", s)
        rights[s, 0] = fetch(right, "y", s)
    for s in (1, 3, 2):
        lefts[s, 0] = fetch(left, "y", s)
        rights[0, s] = fetch(right, "x", s)
    for t in (1, 3, 2):
        for s in (1, 3, 2):
            lefts[s, t] = fetch(lefts[0, t], "y", s)
            rights[t, s] = fetch(rights[t, 0], "x", s)

    all_tokens, projected = pl.pallas_call(
        token_kernel,
        out_shape=[
            jax.ShapeDtypeStruct((4, length, width), BF16),
            jax.ShapeDtypeStruct((length, 8), F32),
        ],
        in_specs=[SMEM] + [VMEM] * 5,
        out_specs=[VMEM] * 2,
        name="member_tokens",
    )(tp.reshape(1), tokens, mate, twin, both, noise_in.reshape(4, 1, width))

    heads = width // HEAD
    strip = pl.BlockSpec((length, LANES), lambda i: (0, i))
    square = pl.BlockSpec((2, length, length), lambda i: (i, 0, 0))
    high, low = pl.pallas_call(
        score_kernel,
        out_shape=[jax.ShapeDtypeStruct((heads, length, length), BF16)] * 2,
        grid=(width // LANES,),
        in_specs=[SMEM, strip, strip, strip],
        out_specs=[square, square],
        name="decayed_scores",
    )(live_length, receptance, keys, log_decay)

    population = lax.axis_size("pop")
    weighted = noise_in.astype(F32) * (utilities / math.sqrt(population))[:, None]
    message = jnp.concatenate(
        [
            weighted.reshape(population, rows),
            jnp.zeros((population, LANES - rows), F32),
            jnp.broadcast_to(noise_out.astype(F32), (population, width)),
        ],
        1,
    )
    message = lax.all_to_all(message, "pop", split_axis=0, concat_axis=0, tiled=True)
    update = lax.dot_general(
        message[:, :rows],
        message[:, LANES:],
        (((0,), (0,)), ((), ())),
        precision=HIGHEST,
        preferred_element_type=F32,
    )

    order = [(a, b) for a in range(SIDE) for b in range(SIDE)]
    wkv_out = pl.pallas_call(
        functools.partial(readout_kernel, len(order)),
        out_shape=jax.ShapeDtypeStruct((length, width), BF16),
        in_specs=[SMEM] + [VMEM] * (2 * len(order) + 5),
        out_specs=VMEM,
        compiler_params=params(40),
        name="values_readout",
    )(
        jnp.stack([y, x]),
        *[lefts[k] for k in order],
        *[rights[k] for k in order],
        all_tokens,
        projected,
        noise_out,
        high,
        low,
    )
    return wkv_out.reshape(1, length, width), update


def solution(mesh):
    return jax.shard_map(
        body,
        mesh=mesh,
        in_specs=(
            P("pop", None, "tp"),
            P("pop", None, "tp"),
            P("pop", None, "tp"),
            P("pop", None, "tp"),
            P("pop", "tp"),
            P("pop", None),
            P("pop", "tp"),
            P("pop"),
            P("pop"),
        ),
        out_specs=(P("pop", None, "tp"), P("pop", "tp")),
        check_vma=False,
    )
```

```python
import functools
import math

import jax
import jax.numpy as jnp
from jax import lax
from jax.experimental import pallas as pl
from jax.experimental.pallas import tpu as pltpu
from jax.sharding import PartitionSpec as P

HEAD = 64
SIGMA = 0.5
HIGHEST = lax.Precision.HIGHEST
F32 = jnp.float32
BF16 = jnp.bfloat16

SIDE = 4
STRIDE = {"y": 16, "x": 4, "z": 1}
SPAN = 64
LANES = 128

VMEM = pl.BlockSpec(memory_space=pltpu.VMEM)
ANY = pl.BlockSpec(memory_space=pl.ANY)
SMEM = pl.BlockSpec(memory_space=pltpu.SMEM)


def fetch(array, axis, step):
    stride = STRIDE[axis]
    pairs = []
    for me in range(SIDE**3):
        at = (me // stride) % SIDE
        pairs.append((me + ((at + step) % SIDE - at) * stride, me))
    return lax.ppermute(array, "pop", pairs)


def swap(array, bit):
    return lax.ppermute(array, "tp", [(i, i ^ bit) for i in range(4)])


def score_kernel(live_ref, recept_ref, keys_ref, decay_ref, high_ref, low_ref):
    length = recept_ref.shape[0]
    live = live_ref[0]
    row = lax.broadcasted_iota(jnp.int32, (length, LANES), 0)
    alive = row < live
    decay = jnp.where(alive, decay_ref[...], jnp.zeros((), BF16))
    keys = jnp.where(alive, keys_ref[...].astype(F32), 0.0)
    lower = (
        lax.broadcasted_iota(jnp.int32, (length, length), 0)
        >= lax.broadcasted_iota(jnp.int32, (length, length), 1)
    ).astype(F32).astype(BF16)
    summed = jnp.dot(lower, decay, preferred_element_type=F32)
    lane = lax.broadcasted_iota(jnp.int32, (SPAN, LANES), 1)
    for chunk in range(length // SPAN):
        first, last = chunk * SPAN, (chunk + 1) * SPAN
        base = summed[first - 1 : first] if chunk else jnp.zeros((1, LANES), F32)
        grown = recept_ref[first:last].astype(F32) * jnp.exp(summed[first:last] - base)
        shrunk = keys[:last] * jnp.exp(base - summed[:last])
        both = jnp.concatenate(
            [jnp.where(lane < HEAD, grown, 0.0), jnp.where(lane < HEAD, 0.0, grown)], 0
        )
        scores = lax.dot_general(
            both, shrunk, (((1,), (1,)), ((), ())), precision=HIGHEST, preferred_element_type=F32
        )
        for head in range(2):
            mine = scores[head * SPAN : (head + 1) * SPAN]
            here = lax.broadcasted_iota(jnp.int32, (SPAN, last), 0) + first
            there = lax.broadcasted_iota(jnp.int32, (SPAN, last), 1)
            mine = jnp.where((here >= there) & (here < live), mine, 0.0)
            high = mine.astype(BF16)
            low = (mine - high.astype(F32)).astype(BF16)
            high_ref[head, first:last, :last] = high
            low_ref[head, first:last, :last] = low
            if last < length:
                rest = jnp.zeros((SPAN, length - last), BF16)
                high_ref[head, first:last, last:] = rest
                low_ref[head, first:last, last:] = rest


def join_kernel(pop_ref, p0, p1, p2, p3, left_ref, right_ref, sems):
    rows = p0.shape[0]
    half = left_ref.shape[1]
    copies = []
    for step, part in enumerate((p0, p1, p2, p3)):
        place = pl.ds(pl.multiple_of(lax.rem(pop_ref[0] + step, SIDE) * rows, rows), rows)
        for side, out in enumerate((left_ref, right_ref)):
            copies.append(
                pltpu.make_async_copy(
                    part.at[:, side * half : (side + 1) * half], out.at[place], sems.at[step, side]
                )
            )
    for copy in copies:
        copy.start()
    for copy in copies:
        copy.wait()


def join_rows(pop, parts):
    rows, width = parts[0].shape
    return pl.pallas_call(
        join_kernel,
        out_shape=[jax.ShapeDtypeStruct((SIDE * rows, width // 2), BF16)] * 2,
        in_specs=[SMEM] + [ANY] * 4,
        out_specs=[ANY] * 2,
        scratch_shapes=[pltpu.SemaphoreType.DMA((SIDE, 2))],
        name="join_rows",
    )(pop, *parts)


def stack_kernel(*refs):
    parts, out_ref, sems = refs[:-2], refs[-2], refs[-1]
    rows = parts[0].shape[0]
    copies = [
        pltpu.make_async_copy(part, out_ref.at[i * rows : (i + 1) * rows], sems.at[i])
        for i, part in enumerate(parts)
    ]
    for copy in copies:
        copy.start()
    for copy in copies:
        copy.wait()


def stack_rows(parts):
    rows, width = parts[0].shape
    return pl.pallas_call(
        stack_kernel,
        out_shape=jax.ShapeDtypeStruct((len(parts) * rows, width), BF16),
        in_specs=[ANY] * len(parts),
        out_specs=ANY,
        scratch_shapes=[pltpu.SemaphoreType.DMA((len(parts),))],
        name="stack_rows",
    )(*parts)


def token_kernel(at_ref, t0, t1, t2, t3, noise_ref, tokens_ref, projected_ref):
    total = None
    for bits, part in enumerate((t0, t1, t2, t3)):
        place = jnp.bitwise_xor(at_ref[0], bits)
        block = part[...]
        tokens_ref[place] = block
        noise = jnp.broadcast_to(noise_ref[place], (8, block.shape[1]))
        term = lax.dot_general(
            block, noise, (((1,), (1,)), ((), ())), preferred_element_type=F32
        )
        total = term if total is None else total + term
    projected_ref[...] = total


def token_blocks(pop_ref, tokens_ref, side, far, nears):
    y, x = lax.div(pop_ref[0], SIDE * SIDE), lax.rem(lax.div(pop_ref[0], SIDE), SIDE)
    depth = tokens_ref.shape[2] // SIDE
    blocks = []
    for near in nears:
        dy, dx = (far, near) if side == 0 else (near, far)
        place = pl.ds(pl.multiple_of(lax.rem(x + dx, SIDE) * depth, depth), depth)
        blocks.append(tokens_ref[lax.rem(y + dy, SIDE), :, place])
    return jnp.concatenate(blocks, 1)


def product_kernel(plan, added, pop_ref, tokens_ref, *refs):
    refs = list(refs)
    sum_ref = refs.pop(0) if added else None
    count = len(plan)
    pieces, out_ref, held, sems = refs[:count], refs[count], refs[count + 1], refs[count + 2]
    half = out_ref.shape[1] // 2
    copies = [pltpu.make_async_copy(p, held.at[i], sems.at[i]) for i, p in enumerate(pieces)]
    for copy in copies:
        copy.start()
    totals = [None, None]
    for i, (side, far, nears) in enumerate(plan):
        blocks = token_blocks(pop_ref, tokens_ref, side, far, nears)
        copies[i].wait()
        term = jnp.dot(blocks, held[i], preferred_element_type=F32)
        totals[side] = term if totals[side] is None else totals[side] + term
    for side in range(2):
        where = slice(side * half, (side + 1) * half)
        total = totals[side]
        if added:
            total = total + sum_ref[:, where]
        out_ref[:, where] = total


def product(pop, tokens, plan, pieces, before=None):
    length, width = tokens.shape[1:]
    extra = () if before is None else (before,)
    return pl.pallas_call(
        functools.partial(product_kernel, plan, before is not None),
        out_shape=jax.ShapeDtypeStruct((length, width), F32),
        in_specs=[SMEM, VMEM] + [VMEM] * len(extra) + [ANY] * len(pieces),
        out_specs=VMEM,
        scratch_shapes=[
            pltpu.VMEM((len(pieces),) + pieces[0].shape, BF16),
            pltpu.SemaphoreType.DMA((len(pieces),)),
        ],
        compiler_params=params(24),
        cost_estimate=pl.CostEstimate(
            flops=len(pieces) * 2 * length * pieces[0].size,
            bytes_accessed=len(pieces) * 2 * pieces[0].size + 4 * length * width * 2,
            transcendentals=0,
        ),
        name="products",
    )(pop, tokens, *extra, *pieces)


def readout_kernel(plan, pop_ref, *refs):
    count = len(plan)
    tokens_ref, sum_ref, projected_ref, noise_ref, high_ref, low_ref = refs[:6]
    pieces = refs[6 : 6 + count]
    out_ref, held, sems = refs[6 + count :]
    half = out_ref.shape[1] // 2
    copies = [pltpu.make_async_copy(p, held.at[i], sems.at[i]) for i, p in enumerate(pieces)]
    for copy in copies:
        copy.start()
    projected = projected_ref[...][:, :1] * (SIGMA / math.sqrt(SIDE**3 * 64))
    lane = lax.broadcasted_iota(jnp.int32, (out_ref.shape[0], LANES), 1)
    for side in range(2):
        where = slice(side * half, (side + 1) * half)
        total = sum_ref[:, where] + projected * noise_ref[:, where].astype(F32)
        for i, (at, far, nears) in enumerate(plan):
            if at == side:
                blocks = token_blocks(pop_ref, tokens_ref, side, far, nears)
                copies[i].wait()
                total = total + jnp.dot(blocks, held[i], preferred_element_type=F32)
        values = total.astype(BF16)
        for pair in range(half // LANES):
            mine = values[:, pair * LANES : (pair + 1) * LANES]
            head = side * (half // HEAD) + 2 * pair
            outs = [
                jnp.dot(high_ref[head + i], mine, preferred_element_type=F32)
                + jnp.dot(low_ref[head + i], mine, preferred_element_type=F32)
                for i in range(2)
            ]
            start = side * half + pair * LANES
            out_ref[:, start : start + LANES] = jnp.where(lane < HEAD, *outs).astype(BF16)


def params(mib):
    return pltpu.CompilerParams(vmem_limit_bytes=mib << 20)


def after(value, *others):
    return lax.optimization_barrier((value, others))[0]


def body(
    tokens, receptance, keys, log_decay, value_weight, noise_in, noise_out, utilities, live_length
):
    _, length, width = receptance.shape
    pop = lax.axis_index("pop").reshape(1)
    tp = lax.axis_index("tp").reshape(1)
    tokens, receptance, keys, log_decay = (
        a.reshape(length, width) for a in (tokens, receptance, keys, log_decay)
    )
    rows = value_weight.shape[0]

    population = lax.axis_size("pop")
    weighted = noise_in.astype(F32) * (utilities / math.sqrt(population))[:, None]
    message = jnp.concatenate(
        [
            weighted.reshape(population, rows),
            jnp.zeros((population, LANES - rows), F32),
            jnp.broadcast_to(noise_out.astype(F32), (population, width)),
        ],
        1,
    )
    message = lax.all_to_all(message, "pop", split_axis=0, concat_axis=0, tiled=True)

    parts = [value_weight] + [fetch(value_weight, "z", s) for s in (1, 2, 3)]
    left, right = join_rows(pop, parts)

    twin = swap(after(tokens, left), 2)

    lefts, rights = {0: left}, {0: right}
    for s in (1, 3):
        lefts[s] = fetch(left, "x", s)
        rights[s] = fetch(right, "y", s)
    for s in (2,):
        lefts[s] = fetch(left, "x", s)
        rights[s] = fetch(right, "y", s)
    left = stack_rows([lefts[s] for s in range(SIDE)])
    right = stack_rows([rights[s] for s in range(SIDE)])

    l1, l3 = fetch(left, "y", 1), fetch(left, "y", 3)
    r1, r3 = fetch(right, "x", 1), fetch(right, "x", 3)

    mate = swap(after(tokens, twin), 1)
    both = swap(twin, 1)
    all_tokens, projected = pl.pallas_call(
        token_kernel,
        out_shape=[
            jax.ShapeDtypeStruct((4, length, width), BF16),
            jax.ShapeDtypeStruct((length, 8), F32),
        ],
        in_specs=[SMEM] + [VMEM] * 5,
        out_specs=[VMEM] * 2,
        cost_estimate=pl.CostEstimate(flops=0, bytes_accessed=8 << 20, transcendentals=0),
        name="member_tokens",
    )(tp, tokens, mate, twin, both, noise_in.reshape(4, 1, width))

    heads = width // HEAD
    strip = pl.BlockSpec((length, LANES), lambda i: (0, i))
    square = pl.BlockSpec((2, length, length), lambda i: (i, 0, 0))
    recept = after(receptance, left, right)
    high, low = pl.pallas_call(
        score_kernel,
        out_shape=[jax.ShapeDtypeStruct((heads, length, length), BF16)] * 2,
        grid=(width // LANES,),
        in_specs=[SMEM, strip, strip, strip],
        out_specs=[square, square],
        cost_estimate=pl.CostEstimate(flops=0, bytes_accessed=24 << 20, transcendentals=0),
        name="decayed_scores",
    )(live_length, recept, keys, log_decay)

    update = lax.dot_general(
        message[:, :rows],
        message[:, LANES:],
        (((0,), (0,)), ((), ())),
        precision=HIGHEST,
        preferred_element_type=F32,
    )
    every = tuple(range(SIDE))
    total = product(pop, all_tokens, ((0, 0, every), (1, 0, every)), (left, right))

    middle = l1.shape[0] // 2
    l1, l3, r1, r3, high, low, update = lax.optimization_barrier(
        (l1, l3, r1, r3, high, low, update)
    )
    l2a, l2b = fetch(l1[:middle], "y", 1), fetch(l3[middle:], "y", 3)
    r2a, r2b = fetch(r1[:middle], "x", 1), fetch(r3[middle:], "x", 3)

    total = product(
        pop,
        all_tokens,
        ((0, 1, every), (0, 3, every), (1, 1, every), (1, 3, every)),
        (l1, l3, r1, r3),
        total,
    )
    plan = ((0, 2, (0, 1)), (0, 2, (2, 3)), (1, 2, (0, 1)), (1, 2, (2, 3)))
    pieces = (l2a, l2b, r2a, r2b)
    wkv_out = pl.pallas_call(
        functools.partial(readout_kernel, plan),
        out_shape=jax.ShapeDtypeStruct((length, width), BF16),
        in_specs=[SMEM] + [VMEM] * 6 + [ANY] * 4,
        out_specs=VMEM,
        scratch_shapes=[
            pltpu.VMEM((4,) + pieces[0].shape, BF16),
            pltpu.SemaphoreType.DMA((4,)),
        ],
        compiler_params=params(24),
        name="values_readout",
    )(pop, all_tokens, total, projected, noise_out, high, low, *pieces)
    return wkv_out.reshape(1, length, width), update


def solution(mesh):
    return jax.shard_map(
        body,
        mesh=mesh,
        in_specs=(
            P("pop", None, "tp"),
            P("pop", None, "tp"),
            P("pop", None, "tp"),
            P("pop", None, "tp"),
            P("pop", "tp"),
            P("pop", None),
            P("pop", "tp"),
            P("pop"),
            P("pop"),
        ),
        out_specs=(P("pop", None, "tp"), P("pop", "tp")),
        check_vma=False,
    )
```

```python
import functools
import math

import jax
import jax.numpy as jnp
from jax import lax
from jax.experimental import pallas as pl
from jax.experimental.pallas import tpu as pltpu
from jax.sharding import Mesh, PartitionSpec as P

HEAD = 64
SIGMA = 0.5
HIGHEST = lax.Precision.HIGHEST
F32 = jnp.float32
BF16 = jnp.bfloat16

SIDE = 4
SPAN = 64
LANES = 128
POP = ("y", "x", "z")
TP = ("twin", "core")

LINKS = {"a": ("x", 1), "b": ("x", 3), "c": ("y", 1), "d": ("y", 3)}
ROUTES = ("acbd", "cadb", "bdac", "dbca")

VMEM = pl.BlockSpec(memory_space=pltpu.VMEM)
SMEM = pl.BlockSpec(memory_space=pltpu.SMEM)


def swap(array, axis, mask):
    size = lax.axis_size(axis)
    return lax.ppermute(array, axis, [(i, i ^ mask) for i in range(size)])


def fetch(array, axis, step):
    size = lax.axis_size(axis)
    return lax.ppermute(array, axis, [((i + step) % size, i) for i in range(size)])


def masks(route, last):
    steps = [LINKS[s] for s in route]
    found = []
    for i in range(2 ** (len(steps) - 1)):
        y = x = 0
        for k, (axis, mask) in enumerate(steps):
            if (i >> k) & 1 or (last and k == len(steps) - 1):
                y, x = (y ^ mask, x) if axis == "y" else (y, x ^ mask)
        found.append((y, x))
    return found


def token_kernel(at_ref, t0, t1, t2, t3, noise_ref, tokens_ref, projected_ref):
    total = None
    for bits, part in enumerate((t0, t1, t2, t3)):
        place = jnp.bitwise_xor(at_ref[0], bits)
        block = part[...]
        tokens_ref[place] = block
        noise = jnp.broadcast_to(noise_ref[place], (8, block.shape[1]))
        term = lax.dot_general(
            block, noise, (((1,), (1,)), ((), ())), preferred_element_type=F32
        )
        total = term if total is None else total + term
    projected_ref[...] = total


def score_kernel(live_ref, recept_ref, keys_ref, decay_ref, high_ref, low_ref):
    length = recept_ref.shape[0]
    live = live_ref[0]
    row = lax.broadcasted_iota(jnp.int32, (length, LANES), 0)
    alive = row < live
    decay = jnp.where(alive, decay_ref[...], jnp.zeros((), BF16))
    keys = jnp.where(alive, keys_ref[...].astype(F32), 0.0)
    lower = (
        lax.broadcasted_iota(jnp.int32, (length, length), 0)
        >= lax.broadcasted_iota(jnp.int32, (length, length), 1)
    ).astype(F32).astype(BF16)
    summed = jnp.dot(lower, decay, preferred_element_type=F32)
    lane = lax.broadcasted_iota(jnp.int32, (SPAN, LANES), 1)
    for chunk in range(length // SPAN):
        first, last = chunk * SPAN, (chunk + 1) * SPAN
        base = summed[first - 1 : first] if chunk else jnp.zeros((1, LANES), F32)
        grown = recept_ref[first:last].astype(F32) * jnp.exp(summed[first:last] - base)
        shrunk = keys[:last] * jnp.exp(base - summed[:last])
        both = jnp.concatenate(
            [jnp.where(lane < HEAD, grown, 0.0), jnp.where(lane < HEAD, 0.0, grown)], 0
        )
        scores = lax.dot_general(
            both, shrunk, (((1,), (1,)), ((), ())), precision=HIGHEST, preferred_element_type=F32
        )
        for head in range(2):
            mine = scores[head * SPAN : (head + 1) * SPAN]
            here = lax.broadcasted_iota(jnp.int32, (SPAN, last), 0) + first
            there = lax.broadcasted_iota(jnp.int32, (SPAN, last), 1)
            mine = jnp.where((here >= there) & (here < live), mine, 0.0)
            high = mine.astype(BF16)
            low = (mine - high.astype(F32)).astype(BF16)
            high_ref[head, first:last, :last] = high
            low_ref[head, first:last, :last] = low
            if last < length:
                rest = jnp.zeros((SPAN, length - last), BF16)
                high_ref[head, first:last, last:] = rest
                low_ref[head, first:last, last:] = rest


def chunk_product(at_ref, tokens_ref, piece_ref, blocks):
    depth = piece_ref.shape[0] // len(blocks)
    group = 4
    total = None
    for first in range(0, len(blocks), group):
        columns = []
        for y, x in blocks[first : first + group]:
            place = pl.multiple_of(jnp.bitwise_xor(at_ref[1], x) * depth, depth)
            columns.append(tokens_ref[jnp.bitwise_xor(at_ref[0], y), :, pl.ds(place, depth)])
        term = jnp.dot(
            jnp.concatenate(columns, 1),
            piece_ref[first * depth : (first + group) * depth],
            preferred_element_type=F32,
        )
        total = term if total is None else total + term
    return total


def held_kernel(at_ref, tokens_ref, *refs):
    pieces, out_ref = refs[:-1], refs[-1]
    wide = pieces[0].shape[1]
    for c, piece in enumerate(pieces):
        out_ref[:, c * wide : (c + 1) * wide] = chunk_product(
            at_ref, tokens_ref, piece, masks(ROUTES[c], False)
        )


def readout_kernel(at_ref, tokens_ref, sum_ref, projected_ref, noise_ref, high_ref, low_ref, *refs):
    pieces, out_ref = refs[:-1], refs[-1]
    wide = pieces[0].shape[1]
    projected = projected_ref[...][:, :1] * (
        SIGMA / math.sqrt(tokens_ref.shape[0] * tokens_ref.shape[2])
    )
    lane = lax.broadcasted_iota(jnp.int32, (out_ref.shape[0], LANES), 1)
    for c, piece in enumerate(pieces):
        where = slice(c * wide, (c + 1) * wide)
        total = sum_ref[:, where] + projected * noise_ref[:, where].astype(F32)
        total = total + chunk_product(at_ref, tokens_ref, piece, masks(ROUTES[c], True))
        values = total.astype(BF16)
        for pair in range(wide // LANES):
            mine = values[:, pair * LANES : (pair + 1) * LANES]
            head = c * (wide // HEAD) + 2 * pair
            outs = [
                jnp.dot(high_ref[head + i], mine, preferred_element_type=F32)
                + jnp.dot(low_ref[head + i], mine, preferred_element_type=F32)
                for i in range(2)
            ]
            start = c * wide + pair * LANES
            out_ref[:, start : start + LANES] = jnp.where(lane < HEAD, *outs).astype(BF16)


def params(mib):
    return pltpu.CompilerParams(vmem_limit_bytes=mib << 20)


def cost(flops, moved):
    return pl.CostEstimate(flops=flops, bytes_accessed=moved, transcendentals=0)


def after(value, *others):
    return lax.optimization_barrier((value, others))[0]


def body(
    tokens, receptance, keys, log_decay, value_weight, noise_in, noise_out, utilities, live_length
):
    _, length, width = receptance.shape
    tokens, receptance, keys, log_decay = (
        a.reshape(length, width) for a in (tokens, receptance, keys, log_decay)
    )
    rows = value_weight.shape[0]
    wide = width // len(ROUTES)

    z = lax.axis_index("z")
    near = jnp.zeros((SIDE * rows, width), BF16)
    for step in (0, 1, 3, 2):
        part = fetch(value_weight, "z", step) if step else value_weight
        near = lax.dynamic_update_slice(near, part, (lax.rem(z + step, SIDE) * rows, 0))

    population = lax.axis_size(POP)
    weighted = noise_in.astype(F32) * (utilities / math.sqrt(population))[:, None]
    message = jnp.concatenate(
        [
            weighted.reshape(population, rows),
            jnp.zeros((population, LANES - rows), F32),
            jnp.broadcast_to(noise_out.astype(F32), (population, width)),
        ],
        1,
    )
    message = lax.all_to_all(message, POP, split_axis=0, concat_axis=0, tiled=True)

    twin = swap(after(tokens, near), "twin", 1)

    held = [near[:, c * wide : (c + 1) * wide] for c in range(len(ROUTES))]
    for step in range(3):
        if step == 2:
            held, message = lax.optimization_barrier((held, message))
        came = [swap(held[c], *LINKS[ROUTES[c][step]]) for c in range(len(ROUTES))]
        held = [jnp.concatenate([a, b], 0) for a, b in zip(held, came)]
    came = [swap(held[c], *LINKS[ROUTES[c][3]]) for c in range(len(ROUTES))]

    mate = swap(after(tokens, twin), "core", 1)
    both = swap(twin, "core", 1)
    tp = lax.axis_index(TP).reshape(1)
    all_tokens, projected = pl.pallas_call(
        token_kernel,
        out_shape=[
            jax.ShapeDtypeStruct((4, length, width), BF16),
            jax.ShapeDtypeStruct((length, 8), F32),
        ],
        in_specs=[SMEM] + [VMEM] * 5,
        out_specs=[VMEM] * 2,
        cost_estimate=cost(0, 8 << 20),
        compiler_params=params(16),
        name="member_tokens",
    )(tp, tokens, mate, twin, both, noise_in.reshape(4, 1, width))

    heads = width // HEAD
    strip = pl.BlockSpec((length, LANES), lambda i: (0, i))
    square = pl.BlockSpec((2, length, length), lambda i: (i, 0, 0))
    high, low = pl.pallas_call(
        score_kernel,
        out_shape=[jax.ShapeDtypeStruct((heads, length, length), BF16)] * 2,
        grid=(width // LANES,),
        in_specs=[SMEM, strip, strip, strip],
        out_specs=[square, square],
        cost_estimate=cost(0, 24 << 20),
        compiler_params=params(16),
        name="decayed_scores",
    )(live_length, after(receptance, *held), keys, log_decay)

    update = lax.dot_general(
        message[:, :rows],
        message[:, LANES:],
        (((0,), (0,)), ((), ())),
        precision=HIGHEST,
        preferred_element_type=F32,
    )

    at = jnp.stack([lax.axis_index("y"), lax.axis_index("x")])
    flops = length * width * 2 * 2048
    total = pl.pallas_call(
        held_kernel,
        out_shape=jax.ShapeDtypeStruct((length, width), F32),
        in_specs=[SMEM] + [VMEM] * 5,
        out_specs=VMEM,
        cost_estimate=cost(flops, 8 << 20),
        compiler_params=params(16),
        name="held_products",
    )(at, all_tokens, *held)
    wkv_out = pl.pallas_call(
        readout_kernel,
        out_shape=jax.ShapeDtypeStruct((length, width), BF16),
        in_specs=[SMEM] + [VMEM] * 10,
        out_specs=VMEM,
        cost_estimate=cost(flops, 12 << 20),
        compiler_params=params(20),
        name="values_readout",
    )(at, all_tokens, total, projected, noise_out, high, low, *came)
    return wkv_out.reshape(1, length, width), update


def solution(mesh):
    mesh = Mesh(mesh.devices.reshape(SIDE, SIDE, SIDE, 2, 2), POP + TP)
    return jax.shard_map(
        body,
        mesh=mesh,
        in_specs=(
            P(POP, None, TP),
            P(POP, None, TP),
            P(POP, None, TP),
            P(POP, None, TP),
            P(POP, TP),
            P(POP, None),
            P(POP, TP),
            P(POP),
            P(POP),
        ),
        out_specs=(P(POP, None, TP), P(POP, TP)),
        check_vma=False,
    )
```

```python
import functools
import math

import jax
import jax.numpy as jnp
from jax import lax
from jax.experimental import pallas as pl
from jax.experimental.pallas import tpu as pltpu
from jax.sharding import Mesh, PartitionSpec as P

HEAD = 64
SIGMA = 0.5
HIGHEST = lax.Precision.HIGHEST
F32 = jnp.float32
BF16 = jnp.bfloat16

SIDE = 4
SPAN = 64
LANES = 128
POP = ("y", "x", "z")
TP = ("twin", "core")

LINKS = {"a": ("x", 1), "b": ("x", 3), "c": ("y", 1), "d": ("y", 3)}
ROUTES = ("acbd", "cadb", "bdac", "dbca")

ANY = pl.BlockSpec(memory_space=pl.ANY)
VMEM = pl.BlockSpec(memory_space=pltpu.VMEM)
SMEM = pl.BlockSpec(memory_space=pltpu.SMEM)


def swap(array, axis, mask):
    size = lax.axis_size(axis)
    return lax.ppermute(array, axis, [(i, i ^ mask) for i in range(size)])


def fetch(array, axis, step):
    size = lax.axis_size(axis)
    return lax.ppermute(array, axis, [((i + step) % size, i) for i in range(size)])


def masks(route, steps):
    found = []
    for i in range(4):
        y = x = 0
        for link in [route[k] for k in range(2) if (i >> k) & 1] + [route[k] for k in steps]:
            axis, mask = LINKS[link]
            y, x = (y ^ mask, x) if axis == "y" else (y, x ^ mask)
        found.append((y, x))
    return found


def token_kernel(at_ref, t0, t1, t2, t3, noise_ref, tokens_ref, projected_ref):
    total = None
    for bits, part in enumerate((t0, t1, t2, t3)):
        place = jnp.bitwise_xor(at_ref[0], bits)
        block = part[...]
        tokens_ref[place] = block
        noise = jnp.broadcast_to(noise_ref[place], (8, block.shape[1]))
        term = lax.dot_general(
            block, noise, (((1,), (1,)), ((), ())), preferred_element_type=F32
        )
        total = term if total is None else total + term
    projected_ref[...] = total


def score_kernel(live_ref, recept_ref, keys_ref, decay_ref, high_ref, low_ref):
    length = recept_ref.shape[0]
    live = live_ref[0]
    row = lax.broadcasted_iota(jnp.int32, (length, LANES), 0)
    alive = row < live
    decay = jnp.where(alive, decay_ref[...], jnp.zeros((), BF16))
    keys = jnp.where(alive, keys_ref[...].astype(F32), 0.0)
    lower = (
        lax.broadcasted_iota(jnp.int32, (length, length), 0)
        >= lax.broadcasted_iota(jnp.int32, (length, length), 1)
    ).astype(F32).astype(BF16)
    summed = jnp.dot(lower, decay, preferred_element_type=F32)
    lane = lax.broadcasted_iota(jnp.int32, (SPAN, LANES), 1)
    for chunk in range(length // SPAN):
        first, last = chunk * SPAN, (chunk + 1) * SPAN
        base = summed[first - 1 : first] if chunk else jnp.zeros((1, LANES), F32)
        grown = recept_ref[first:last].astype(F32) * jnp.exp(summed[first:last] - base)
        shrunk = keys[:last] * jnp.exp(base - summed[:last])
        both = jnp.concatenate(
            [jnp.where(lane < HEAD, grown, 0.0), jnp.where(lane < HEAD, 0.0, grown)], 0
        )
        scores = lax.dot_general(
            both, shrunk, (((1,), (1,)), ((), ())), precision=HIGHEST, preferred_element_type=F32
        )
        for head in range(2):
            mine = scores[head * SPAN : (head + 1) * SPAN]
            here = lax.broadcasted_iota(jnp.int32, (SPAN, last), 0) + first
            there = lax.broadcasted_iota(jnp.int32, (SPAN, last), 1)
            mine = jnp.where((here >= there) & (here < live), mine, 0.0)
            high = mine.astype(BF16)
            low = (mine - high.astype(F32)).astype(BF16)
            high_ref[head, first:last, :last] = high
            low_ref[head, first:last, :last] = low
            if last < length:
                rest = jnp.zeros((SPAN, length - last), BF16)
                high_ref[head, first:last, last:] = rest
                low_ref[head, first:last, last:] = rest


def chunk_product(at_ref, tokens_ref, piece, blocks):
    depth = piece.shape[0] // len(blocks)
    columns = []
    for y, x in blocks:
        place = pl.multiple_of(jnp.bitwise_xor(at_ref[1], x) * depth, depth)
        columns.append(tokens_ref[jnp.bitwise_xor(at_ref[0], y), :, pl.ds(place, depth)])
    return jnp.dot(jnp.concatenate(columns, 1), piece[...], preferred_element_type=F32)


def copies_of(pieces, held, sems):
    copies = [pltpu.make_async_copy(p, held.at[i], sems.at[i]) for i, p in enumerate(pieces)]
    for copy in copies:
        copy.start()
    return copies


def product_kernel(ways, added, at_ref, tokens_ref, *refs):
    refs = list(refs)
    sum_ref = refs.pop(0) if added else None
    out_ref, held, sems = refs[-3:]
    wide = held.shape[2]
    copies = copies_of(refs[:-3], held, sems)
    for c, route in enumerate(ROUTES):
        where = slice(c * wide, (c + 1) * wide)
        total = sum_ref[:, where] if added else None
        for i, steps in enumerate(ways):
            at = c * len(ways) + i
            copies[at].wait()
            term = chunk_product(at_ref, tokens_ref, held.at[at], masks(route, steps))
            total = term if total is None else total + term
        out_ref[:, where] = total


def product(at, tokens, ways, pieces, before=None):
    length, width = tokens.shape[1:]
    extra = () if before is None else (before,)
    return pl.pallas_call(
        functools.partial(product_kernel, ways, before is not None),
        out_shape=jax.ShapeDtypeStruct((length, width), F32),
        in_specs=[SMEM, VMEM] + [VMEM] * len(extra) + [ANY] * len(pieces),
        out_specs=VMEM,
        scratch_shapes=[
            pltpu.VMEM((len(pieces),) + pieces[0].shape, BF16),
            pltpu.SemaphoreType.DMA((len(pieces),)),
        ],
        cost_estimate=cost(len(pieces) * 2 * length * pieces[0].size, 8 << 20),
        compiler_params=params(20),
        name="products",
    )(at, tokens, *extra, *pieces)


def readout_kernel(at_ref, tokens_ref, sum_ref, projected_ref, noise_ref, high_ref, low_ref, *refs):
    out_ref, held, sems = refs[-3:]
    wide = held.shape[2]
    copies = copies_of(refs[:-3], held, sems)
    projected = projected_ref[...][:, :1] * (
        SIGMA / math.sqrt(tokens_ref.shape[0] * tokens_ref.shape[2])
    )
    lane = lax.broadcasted_iota(jnp.int32, (out_ref.shape[0], LANES), 1)
    for c, route in enumerate(ROUTES):
        where = slice(c * wide, (c + 1) * wide)
        total = sum_ref[:, where] + projected * noise_ref[:, where].astype(F32)
        copies[c].wait()
        total = total + chunk_product(at_ref, tokens_ref, held.at[c], masks(route, (2, 3)))
        values = total.astype(BF16)
        for pair in range(wide // LANES):
            mine = values[:, pair * LANES : (pair + 1) * LANES]
            head = c * (wide // HEAD) + 2 * pair
            outs = [
                jnp.dot(high_ref[head + i], mine, preferred_element_type=F32)
                + jnp.dot(low_ref[head + i], mine, preferred_element_type=F32)
                for i in range(2)
            ]
            start = c * wide + pair * LANES
            out_ref[:, start : start + LANES] = jnp.where(lane < HEAD, *outs).astype(BF16)


def params(mib):
    return pltpu.CompilerParams(vmem_limit_bytes=mib << 20)


def cost(flops, moved):
    return pl.CostEstimate(flops=flops, bytes_accessed=moved, transcendentals=0)


def after(value, *others):
    return lax.optimization_barrier((value, others))[0]


def body(
    tokens, receptance, keys, log_decay, value_weight, noise_in, noise_out, utilities, live_length
):
    _, length, width = receptance.shape
    tokens, receptance, keys, log_decay = (
        a.reshape(length, width) for a in (tokens, receptance, keys, log_decay)
    )
    rows = value_weight.shape[0]
    wide = width // len(ROUTES)

    heads = width // HEAD
    strip = pl.BlockSpec((length, LANES), lambda i: (0, i))
    square = pl.BlockSpec((2, length, length), lambda i: (i, 0, 0))
    high, low = pl.pallas_call(
        score_kernel,
        out_shape=[jax.ShapeDtypeStruct((heads, length, length), BF16)] * 2,
        grid=(width // LANES,),
        in_specs=[SMEM, strip, strip, strip],
        out_specs=[square, square],
        cost_estimate=cost(0, 24 << 20),
        name="decayed_scores",
    )(live_length, receptance, keys, log_decay)
    z = lax.axis_index("z")
    near = jnp.zeros((SIDE * rows, width), BF16)
    for step in (0, 1, 3, 2):
        part = fetch(value_weight, "z", step) if step else value_weight
        near = lax.dynamic_update_slice(near, part, (lax.rem(z + step, SIDE) * rows, 0))
    mate = swap(tokens, "core", 1)
    near, high, low, mate = lax.optimization_barrier((near, high, low, mate))

    twin = swap(after(tokens, near), "twin", 1)

    chunks = range(len(ROUTES))
    held = [near[:, c * wide : (c + 1) * wide] for c in chunks]
    for step in range(2):
        came = [swap(held[c], *LINKS[ROUTES[c][step]]) for c in chunks]
        held = [jnp.concatenate([a, b], 0) for a, b in zip(held, came)]
    third = [swap(held[c], *LINKS[ROUTES[c][2]]) for c in chunks]
    fourth = [swap(held[c], *LINKS[ROUTES[c][3]]) for c in chunks]
    last = [swap(third[c], *LINKS[ROUTES[c][3]]) for c in chunks]

    both = swap(after(twin, *third), "core", 1)
    tp = lax.axis_index(TP).reshape(1)
    all_tokens, projected = pl.pallas_call(
        token_kernel,
        out_shape=[
            jax.ShapeDtypeStruct((4, length, width), BF16),
            jax.ShapeDtypeStruct((length, 8), F32),
        ],
        in_specs=[SMEM] + [VMEM] * 5,
        out_specs=[VMEM] * 2,
        cost_estimate=cost(0, 8 << 20),
        compiler_params=params(16),
        name="member_tokens",
    )(tp, tokens, mate, twin, both, noise_in.reshape(4, 1, width))

    population = lax.axis_size(POP)
    weighted = noise_in.astype(F32) * (utilities / math.sqrt(population))[:, None]
    message = jnp.concatenate(
        [
            weighted.reshape(population, rows),
            jnp.zeros((population, LANES - rows), F32),
            jnp.broadcast_to(noise_out.astype(F32), (population, width)),
        ],
        1,
    )
    message = lax.all_to_all(
        after(message, *third), POP, split_axis=0, concat_axis=0, tiled=True
    )
    update = lax.dot_general(
        message[:, :rows],
        message[:, LANES:],
        (((0,), (0,)), ((), ())),
        precision=HIGHEST,
        preferred_element_type=F32,
    )

    at = jnp.stack([lax.axis_index("y"), lax.axis_index("x")])
    total = product(
        at, all_tokens, ((), (2,)), [p for c in chunks for p in (held[c], third[c])]
    )
    total = product(at, all_tokens, ((3,),), fourth, total)
    wkv_out = pl.pallas_call(
        readout_kernel,
        out_shape=jax.ShapeDtypeStruct((length, width), BF16),
        in_specs=[SMEM] + [VMEM] * 6 + [ANY] * len(last),
        out_specs=VMEM,
        scratch_shapes=[
            pltpu.VMEM((len(last),) + last[0].shape, BF16),
            pltpu.SemaphoreType.DMA((len(last),)),
        ],
        cost_estimate=cost(length * width * 2 * 1024, 12 << 20),
        compiler_params=params(20),
        name="values_readout",
    )(at, all_tokens, total, projected, noise_out, high, low, *last)
    return wkv_out.reshape(1, length, width), update


def solution(mesh):
    mesh = Mesh(mesh.devices.reshape(SIDE, SIDE, SIDE, 2, 2), POP + TP)
    return jax.shard_map(
        body,
        mesh=mesh,
        in_specs=(
            P(POP, None, TP),
            P(POP, None, TP),
            P(POP, None, TP),
            P(POP, None, TP),
            P(POP, TP),
            P(POP, None),
            P(POP, TP),
            P(POP),
            P(POP),
        ),
        out_specs=(P(POP, None, TP), P(POP, TP)),
        check_vma=False,
    )
```

```python
import functools
import math

import jax
import jax.numpy as jnp
from jax import lax
from jax.experimental import pallas as pl
from jax.experimental.pallas import tpu as pltpu
from jax.sharding import Mesh, PartitionSpec as P

HEAD = 64
SIGMA = 0.5
HIGHEST = lax.Precision.HIGHEST
F32 = jnp.float32
BF16 = jnp.bfloat16

SIDE = 4
SPAN = 64
LANES = 128
POP = ("y", "x", "z")
TP = ("twin", "core")

LINKS = {"a": ("x", 1), "b": ("x", 3), "c": ("y", 1), "d": ("y", 3)}
ROUTES = ("acbd", "cadb", "bdac", "dbca")

ANY = pl.BlockSpec(memory_space=pl.ANY)
VMEM = pl.BlockSpec(memory_space=pltpu.VMEM)
SMEM = pl.BlockSpec(memory_space=pltpu.SMEM)


def swap(array, axis, mask):
    size = lax.axis_size(axis)
    return lax.ppermute(array, axis, [(i, i ^ mask) for i in range(size)])


def fetch(array, axis, step):
    size = lax.axis_size(axis)
    return lax.ppermute(array, axis, [((i + step) % size, i) for i in range(size)])


def masks(route, steps):
    found = []
    for i in range(4):
        y = x = 0
        for link in [route[k] for k in range(2) if (i >> k) & 1] + [route[k] for k in steps]:
            axis, mask = LINKS[link]
            y, x = (y ^ mask, x) if axis == "y" else (y, x ^ mask)
        found.append((y, x))
    return found


def token_kernel(at_ref, t0, t1, t2, t3, noise_ref, tokens_ref, projected_ref):
    total = None
    for bits, part in enumerate((t0, t1, t2, t3)):
        place = jnp.bitwise_xor(at_ref[0], bits)
        block = part[...]
        tokens_ref[place] = block
        noise = jnp.broadcast_to(noise_ref[place], (8, block.shape[1]))
        term = lax.dot_general(
            block, noise, (((1,), (1,)), ((), ())), preferred_element_type=F32
        )
        total = term if total is None else total + term
    projected_ref[...] = total


def halves(value):
    high = value.astype(BF16)
    return high, (value - high.astype(F32)).astype(BF16)


def score_kernel(live_ref, recept_ref, keys_ref, decay_ref, out_ref):
    length = recept_ref.shape[0]
    live = live_ref[0]
    row = lax.broadcasted_iota(jnp.int32, (length, LANES), 0)
    alive = row < live
    decay = jnp.where(alive, decay_ref[...], jnp.zeros((), BF16))
    keys = jnp.where(alive, keys_ref[...].astype(F32), 0.0)
    lower = (
        lax.broadcasted_iota(jnp.int32, (length, length), 0)
        >= lax.broadcasted_iota(jnp.int32, (length, length), 1)
    ).astype(F32).astype(BF16)
    summed = jnp.dot(lower, decay, preferred_element_type=F32)
    lane = lax.broadcasted_iota(jnp.int32, (SPAN, LANES), 1)
    across = (((1,), (1,)), ((), ()))
    for chunk in range(length // SPAN):
        first, last = chunk * SPAN, (chunk + 1) * SPAN
        base = summed[first - 1 : first] if chunk else jnp.zeros((1, LANES), F32)
        grown = recept_ref[first:last].astype(F32) * jnp.exp(summed[first:last] - base)
        shrunk_high, shrunk_low = halves(keys[:last] * jnp.exp(base - summed[:last]))
        both = jnp.concatenate(
            [jnp.where(lane < HEAD, grown, 0.0), jnp.where(lane < HEAD, 0.0, grown)], 0
        )
        both_high, both_low = halves(both)
        scores = lax.dot_general(
            jnp.concatenate([both_high, both_low], 0), shrunk_high, across, preferred_element_type=F32
        )
        scores = (
            scores[: 2 * SPAN]
            + scores[2 * SPAN :]
            + lax.dot_general(both_high, shrunk_low, across, preferred_element_type=F32)
        )
        here = lax.broadcasted_iota(jnp.int32, (SPAN, last), 0) + first
        there = lax.broadcasted_iota(jnp.int32, (SPAN, last), 1)
        kept = (here >= there) & (here < live)
        for head in range(2):
            parts = halves(jnp.where(kept, scores[head * SPAN : (head + 1) * SPAN], 0.0))
            for i, part in enumerate(parts):
                start = (2 * i + head) * length + first
                out_ref[0, start : start + SPAN, :last] = part
                if last < length:
                    out_ref[0, start : start + SPAN, last:] = jnp.zeros((SPAN, length - last), BF16)


def chunk_product(at_ref, tokens_ref, piece, blocks):
    depth = piece.shape[0] // len(blocks)
    columns = []
    for y, x in blocks:
        place = pl.multiple_of(jnp.bitwise_xor(at_ref[1], x) * depth, depth)
        columns.append(tokens_ref[jnp.bitwise_xor(at_ref[0], y), :, pl.ds(place, depth)])
    return jnp.dot(jnp.concatenate(columns, 1), piece[...], preferred_element_type=F32)


def copies_of(pieces, held, sems):
    copies = [pltpu.make_async_copy(p, held.at[i], sems.at[i]) for i, p in enumerate(pieces)]
    for copy in copies:
        copy.start()
    return copies


def product_kernel(ways, added, at_ref, tokens_ref, *refs):
    refs = list(refs)
    sum_ref = refs.pop(0) if added else None
    out_ref, held, sems = refs[-3:]
    wide = held.shape[2]
    copies = copies_of(refs[:-3], held, sems)
    for c, route in enumerate(ROUTES):
        where = slice(c * wide, (c + 1) * wide)
        total = sum_ref[:, where] if added else None
        for i, steps in enumerate(ways):
            at = c * len(ways) + i
            copies[at].wait()
            term = chunk_product(at_ref, tokens_ref, held.at[at], masks(route, steps))
            total = term if total is None else total + term
        out_ref[:, where] = total


def product(at, tokens, ways, pieces, before=None):
    length, width = tokens.shape[1:]
    extra = () if before is None else (before,)
    return pl.pallas_call(
        functools.partial(product_kernel, ways, before is not None),
        out_shape=jax.ShapeDtypeStruct((length, width), F32),
        in_specs=[SMEM, VMEM] + [VMEM] * len(extra) + [ANY] * len(pieces),
        out_specs=VMEM,
        scratch_shapes=[
            pltpu.VMEM((len(pieces),) + pieces[0].shape, BF16),
            pltpu.SemaphoreType.DMA((len(pieces),)),
        ],
        cost_estimate=cost(len(pieces) * 2 * length * pieces[0].size, 8 << 20),
        compiler_params=params(20),
        name="products",
    )(at, tokens, *extra, *pieces)


def readout_kernel(at_ref, tokens_ref, sum_ref, projected_ref, noise_ref, scores_ref, *refs):
    out_ref, held, sems = refs[-3:]
    wide = held.shape[2]
    copies = copies_of(refs[:-3], held, sems)
    projected = projected_ref[...][:, :1] * (
        SIGMA / math.sqrt(tokens_ref.shape[0] * tokens_ref.shape[2])
    )
    length = out_ref.shape[0]
    lane = lax.broadcasted_iota(jnp.int32, (length, LANES), 1)
    for c, route in enumerate(ROUTES):
        where = slice(c * wide, (c + 1) * wide)
        total = sum_ref[:, where] + projected * noise_ref[:, where].astype(F32)
        copies[c].wait()
        total = total + chunk_product(at_ref, tokens_ref, held.at[c], masks(route, (2, 3)))
        values = total.astype(BF16)
        for pair in range(wide // LANES):
            mine = values[:, pair * LANES : (pair + 1) * LANES]
            outs = jnp.dot(
                scores_ref[c * (wide // LANES) + pair], mine, preferred_element_type=F32
            )
            outs = outs[: 2 * length] + outs[2 * length :]
            start = c * wide + pair * LANES
            out_ref[:, start : start + LANES] = jnp.where(
                lane < HEAD, outs[:length], outs[length:]
            ).astype(BF16)


def params(mib):
    return pltpu.CompilerParams(vmem_limit_bytes=mib << 20)


def cost(flops, moved):
    return pl.CostEstimate(flops=flops, bytes_accessed=moved, transcendentals=0)


def after(value, *others):
    return lax.optimization_barrier((value, others))[0]


def score_heads(live_length, receptance, keys, log_decay):
    length, width = receptance.shape
    count = width // LANES
    strip = pl.BlockSpec((length, LANES), lambda i: (0, i))
    return pl.pallas_call(
        score_kernel,
        out_shape=jax.ShapeDtypeStruct((count, 4 * length, length), BF16),
        grid=(count,),
        in_specs=[SMEM, strip, strip, strip],
        out_specs=pl.BlockSpec((1, 4 * length, length), lambda i: (i, 0, 0)),
        cost_estimate=cost(0, 20 << 20),
        name="decayed_scores",
    )(live_length, receptance, keys, log_decay)


def body(
    tokens, receptance, keys, log_decay, value_weight, noise_in, noise_out, utilities, live_length
):
    _, length, width = receptance.shape
    tokens, receptance, keys, log_decay = (
        a.reshape(length, width) for a in (tokens, receptance, keys, log_decay)
    )
    rows = value_weight.shape[0]
    wide = width // len(ROUTES)

    z = lax.axis_index("z")
    near = jnp.zeros((SIDE * rows, width), BF16)
    for step in (0, 1, 3, 2):
        part = fetch(value_weight, "z", step) if step else value_weight
        near = lax.dynamic_update_slice(near, part, (lax.rem(z + step, SIDE) * rows, 0))
    mate = swap(tokens, "core", 1)
    population = lax.axis_size(POP)
    weighted = noise_in.astype(F32) * (utilities / math.sqrt(population))[:, None]
    message = jnp.concatenate(
        [
            weighted.reshape(population, rows),
            jnp.zeros((population, LANES - rows), F32),
            jnp.broadcast_to(noise_out.astype(F32), (population, width)),
        ],
        1,
    )
    scores = score_heads(live_length, receptance, keys, log_decay)
    near, mate, message, scores = lax.optimization_barrier((near, mate, message, scores))

    twin = swap(after(tokens, near), "twin", 1)

    chunks = range(len(ROUTES))
    held = [near[:, c * wide : (c + 1) * wide] for c in chunks]
    for step in range(2):
        came = [swap(held[c], *LINKS[ROUTES[c][step]]) for c in chunks]
        held = [jnp.concatenate([a, b], 0) for a, b in zip(held, came)]
    message = lax.all_to_all(
        after(message, *held), POP, split_axis=0, concat_axis=0, tiled=True
    )
    third = [swap(held[c], *LINKS[ROUTES[c][2]]) for c in chunks]
    fourth = [swap(held[c], *LINKS[ROUTES[c][3]]) for c in chunks]
    ready = list(third)
    ready[3] = after(third[3], message)
    last = [swap(ready[c], *LINKS[ROUTES[c][3]]) for c in chunks]

    both = swap(after(twin, *third), "core", 1)
    tp = lax.axis_index(TP).reshape(1)
    all_tokens, projected = pl.pallas_call(
        token_kernel,
        out_shape=[
            jax.ShapeDtypeStruct((4, length, width), BF16),
            jax.ShapeDtypeStruct((length, 8), F32),
        ],
        in_specs=[SMEM] + [VMEM] * 5,
        out_specs=[VMEM] * 2,
        cost_estimate=cost(0, 8 << 20),
        compiler_params=params(16),
        name="member_tokens",
    )(tp, tokens, mate, twin, both, noise_in.reshape(4, 1, width))

    update = lax.dot_general(
        message[:, :rows],
        message[:, LANES:],
        (((0,), (0,)), ((), ())),
        precision=HIGHEST,
        preferred_element_type=F32,
    )

    at = jnp.stack([lax.axis_index("y"), lax.axis_index("x")])
    total = product(
        at, all_tokens, ((), (2,)), [p for c in chunks for p in (held[c], third[c])]
    )
    total = product(at, all_tokens, ((3,),), fourth, total)
    wkv_out = pl.pallas_call(
        readout_kernel,
        out_shape=jax.ShapeDtypeStruct((length, width), BF16),
        in_specs=[SMEM] + [VMEM] * 5 + [ANY] * len(last),
        out_specs=VMEM,
        scratch_shapes=[
            pltpu.VMEM((len(last),) + last[0].shape, BF16),
            pltpu.SemaphoreType.DMA((len(last),)),
        ],
        cost_estimate=cost(length * width * 2 * 1024, 12 << 20),
        compiler_params=params(20),
        name="values_readout",
    )(at, all_tokens, total, projected, noise_out, scores, *last)
    return wkv_out.reshape(1, length, width), update


def solution(mesh):
    mesh = Mesh(mesh.devices.reshape(SIDE, SIDE, SIDE, 2, 2), POP + TP)
    return jax.shard_map(
        body,
        mesh=mesh,
        in_specs=(
            P(POP, None, TP),
            P(POP, None, TP),
            P(POP, None, TP),
            P(POP, None, TP),
            P(POP, TP),
            P(POP, None),
            P(POP, TP),
            P(POP),
            P(POP),
        ),
        out_specs=(P(POP, None, TP), P(POP, TP)),
        check_vma=False,
    )
```

```python
import functools
import math

import jax
import jax.numpy as jnp
from jax import lax
from jax.experimental import pallas as pl
from jax.experimental.pallas import tpu as pltpu
from jax.sharding import Mesh, PartitionSpec as P

HEAD = 64
SIGMA = 0.5
HIGHEST = lax.Precision.HIGHEST
F32 = jnp.float32
BF16 = jnp.bfloat16

SIDE = 4
SPAN = 64
LANES = 128
POP = ("y", "x", "z")
TP = ("twin", "core")

LINKS = {"a": ("x", 1), "b": ("x", 3), "c": ("y", 1), "d": ("y", 3)}
ROUTES = ("acbd", "cadb", "bdac", "dbca")

ANY = pl.BlockSpec(memory_space=pl.ANY)
VMEM = pl.BlockSpec(memory_space=pltpu.VMEM)
SMEM = pl.BlockSpec(memory_space=pltpu.SMEM)


def swap(array, axis, mask):
    size = lax.axis_size(axis)
    return lax.ppermute(array, axis, [(i, i ^ mask) for i in range(size)])


def fetch(array, axis, step):
    size = lax.axis_size(axis)
    return lax.ppermute(array, axis, [((i + step) % size, i) for i in range(size)])


def masks(route, steps):
    found = []
    for i in range(4):
        y = x = 0
        for link in [route[k] for k in range(2) if (i >> k) & 1] + [route[k] for k in steps]:
            axis, mask = LINKS[link]
            y, x = (y ^ mask, x) if axis == "y" else (y, x ^ mask)
        found.append((y, x))
    return found


def token_kernel(at_ref, t0, t1, t2, t3, noise_ref, tokens_ref, projected_ref):
    total = None
    for bits, part in enumerate((t0, t1, t2, t3)):
        place = jnp.bitwise_xor(at_ref[0], bits)
        block = part[...]
        tokens_ref[place] = block
        noise = jnp.broadcast_to(noise_ref[place], (8, block.shape[1]))
        term = lax.dot_general(
            block, noise, (((1,), (1,)), ((), ())), preferred_element_type=F32
        )
        total = term if total is None else total + term
    projected_ref[...] = total


def halves(value):
    high = value.astype(BF16)
    return high, (value - high.astype(F32)).astype(BF16)


def score_kernel(live_ref, recept_ref, keys_ref, decay_ref, out_ref):
    length = recept_ref.shape[0]
    live = live_ref[0]
    row = lax.broadcasted_iota(jnp.int32, (length, LANES), 0)
    alive = row < live
    decay = jnp.where(alive, decay_ref[...], jnp.zeros((), BF16))
    keys = jnp.where(alive, keys_ref[...].astype(F32), 0.0)
    lower = (
        lax.broadcasted_iota(jnp.int32, (length, length), 0)
        >= lax.broadcasted_iota(jnp.int32, (length, length), 1)
    ).astype(F32).astype(BF16)
    summed = jnp.dot(lower, decay, preferred_element_type=F32)
    lane = lax.broadcasted_iota(jnp.int32, (SPAN, LANES), 1)
    across = (((1,), (1,)), ((), ()))
    for chunk in range(length // SPAN):
        first, last = chunk * SPAN, (chunk + 1) * SPAN
        base = summed[first - 1 : first] if chunk else jnp.zeros((1, LANES), F32)
        grown = recept_ref[first:last].astype(F32) * jnp.exp(summed[first:last] - base)
        shrunk_high, shrunk_low = halves(keys[:last] * jnp.exp(base - summed[:last]))
        both = jnp.concatenate(
            [jnp.where(lane < HEAD, grown, 0.0), jnp.where(lane < HEAD, 0.0, grown)], 0
        )
        both_high, both_low = halves(both)
        scores = lax.dot_general(
            jnp.concatenate([both_high, both_low], 0), shrunk_high, across, preferred_element_type=F32
        )
        scores = (
            scores[: 2 * SPAN]
            + scores[2 * SPAN :]
            + lax.dot_general(both_high, shrunk_low, across, preferred_element_type=F32)
        )
        here = lax.broadcasted_iota(jnp.int32, (SPAN, last), 0) + first
        there = lax.broadcasted_iota(jnp.int32, (SPAN, last), 1)
        kept = (here >= there) & (here < live)
        for head in range(2):
            parts = halves(jnp.where(kept, scores[head * SPAN : (head + 1) * SPAN], 0.0))
            for i, part in enumerate(parts):
                start = (2 * i + head) * length + first
                out_ref[0, start : start + SPAN, :last] = part
                if last < length:
                    out_ref[0, start : start + SPAN, last:] = jnp.zeros((SPAN, length - last), BF16)


def chunk_product(at_ref, tokens_ref, piece, blocks):
    depth = piece.shape[0] // len(blocks)
    columns = []
    for y, x in blocks:
        place = pl.multiple_of(jnp.bitwise_xor(at_ref[1], x) * depth, depth)
        columns.append(tokens_ref[jnp.bitwise_xor(at_ref[0], y), :, pl.ds(place, depth)])
    return jnp.dot(jnp.concatenate(columns, 1), piece[...], preferred_element_type=F32)


def copies_of(pieces, held, sems):
    copies = [pltpu.make_async_copy(p, held.at[i], sems.at[i]) for i, p in enumerate(pieces)]
    for copy in copies:
        copy.start()
    return copies


def product_kernel(ways, added, at_ref, tokens_ref, *refs):
    refs = list(refs)
    sum_ref = refs.pop(0) if added else None
    out_ref, held, sems = refs[-3:]
    wide = held.shape[2]
    copies = copies_of(refs[:-3], held, sems)
    for c, route in enumerate(ROUTES):
        where = slice(c * wide, (c + 1) * wide)
        total = sum_ref[:, where] if added else None
        for i, steps in enumerate(ways):
            at = c * len(ways) + i
            copies[at].wait()
            term = chunk_product(at_ref, tokens_ref, held.at[at], masks(route, steps))
            total = term if total is None else total + term
        out_ref[:, where] = total


def product(at, tokens, ways, pieces, before=None):
    length, width = tokens.shape[1:]
    extra = () if before is None else (before,)
    return pl.pallas_call(
        functools.partial(product_kernel, ways, before is not None),
        out_shape=jax.ShapeDtypeStruct((length, width), F32),
        in_specs=[SMEM, VMEM] + [VMEM] * len(extra) + [ANY] * len(pieces),
        out_specs=VMEM,
        scratch_shapes=[
            pltpu.VMEM((len(pieces),) + pieces[0].shape, BF16),
            pltpu.SemaphoreType.DMA((len(pieces),)),
        ],
        cost_estimate=cost(len(pieces) * 2 * length * pieces[0].size, 8 << 20),
        compiler_params=params(20),
        name="products",
    )(at, tokens, *extra, *pieces)


def readout_kernel(at_ref, tokens_ref, sum_ref, projected_ref, noise_ref, scores_ref, *refs):
    out_ref, held, sems = refs[-3:]
    wide = held.shape[2]
    copies = copies_of(refs[:-3], held, sems)
    projected = projected_ref[...][:, :1] * (
        SIGMA / math.sqrt(tokens_ref.shape[0] * tokens_ref.shape[2])
    )
    length = out_ref.shape[0]
    lane = lax.broadcasted_iota(jnp.int32, (length, LANES), 1)
    for c, route in enumerate(ROUTES):
        where = slice(c * wide, (c + 1) * wide)
        total = sum_ref[:, where] + projected * noise_ref[:, where].astype(F32)
        copies[c].wait()
        total = total + chunk_product(at_ref, tokens_ref, held.at[c], masks(route, (2, 3)))
        values = total.astype(BF16)
        for pair in range(wide // LANES):
            mine = values[:, pair * LANES : (pair + 1) * LANES]
            outs = jnp.dot(
                scores_ref[c * (wide // LANES) + pair], mine, preferred_element_type=F32
            )
            outs = outs[: 2 * length] + outs[2 * length :]
            start = c * wide + pair * LANES
            out_ref[:, start : start + LANES] = jnp.where(
                lane < HEAD, outs[:length], outs[length:]
            ).astype(BF16)


def pack_kernel(utility_ref, weight_ref, noise_in_ref, noise_out_ref, out_ref):
    rows, width = weight_ref.shape
    out_ref[:rows] = weight_ref[...]
    line = lax.broadcasted_iota(jnp.int32, (8, width), 0)
    lane = lax.broadcasted_iota(jnp.int32, (8, width), 1)
    packed = jnp.where(line == 0, noise_out_ref[...].astype(F32), 0.0)
    for i in range(SIDE):
        part = noise_in_ref[:, i * width : (i + 1) * width].astype(F32)
        packed = jnp.where(line == 1 + i, part, packed)
    rest = jnp.full((8, width), utility_ref[0], F32)
    for i in range(3):
        term = rest.astype(BF16).astype(F32)
        packed = jnp.where((line == 5) & (lane == i), term, packed)
        rest = rest - term
    out_ref[rows:] = packed.astype(BF16)


def message_kernel(p0, p1, p2, p3, out_ref):
    rows, width = p0.shape[0] - 8, p0.shape[1]
    wide = width // SIDE
    scale = 1 / math.sqrt(SIDE**3)
    weighted, plain = [], []
    for part in (p0, p1, p2, p3):
        noise = part[rows:].astype(F32)
        utility = (noise[5:6, 0:1] + noise[5:6, 1:2]) + noise[5:6, 2:3]
        weighted.append(noise[1:5] * (utility * scale))
        plain.append(noise[0:1])
    plain = jnp.concatenate(plain, 0)
    for y in range(SIDE):
        line = jnp.concatenate([w[y : y + 1] for w in weighted], 0)
        for x in range(SIDE):
            out_ref[y * SIDE + x, :, :wide] = line[:, x * wide : (x + 1) * wide]
            out_ref[y * SIDE + x, :, wide:] = plain


def update_kernel(z_ref, message_ref, out_ref, held):
    rows, width = out_ref.shape
    wide = message_ref.shape[2] - width
    for i in range(message_ref.shape[0]):
        held[i * SIDE : (i + 1) * SIDE] = message_ref[i]
    weighted = pltpu.roll(held[:, :wide], lax.rem(SIDE - z_ref[0], SIDE) * rows, 1)[:, :LANES]
    out_ref[...] = lax.dot_general(
        weighted,
        held[:, wide:],
        (((0,), (0,)), ((), ())),
        precision=HIGHEST,
        preferred_element_type=F32,
    )[:rows]


def params(mib):
    return pltpu.CompilerParams(vmem_limit_bytes=mib << 20)


def cost(flops, moved):
    return pl.CostEstimate(flops=flops, bytes_accessed=moved, transcendentals=0)


def after(value, *others):
    return lax.optimization_barrier((value, others))[0]


def score_heads(live_length, receptance, keys, log_decay):
    length, width = receptance.shape
    count = width // LANES
    strip = pl.BlockSpec((length, LANES), lambda i: (0, i))
    return pl.pallas_call(
        score_kernel,
        out_shape=jax.ShapeDtypeStruct((count, 4 * length, length), BF16),
        grid=(count,),
        in_specs=[SMEM, strip, strip, strip],
        out_specs=pl.BlockSpec((1, 4 * length, length), lambda i: (i, 0, 0)),
        cost_estimate=cost(0, 20 << 20),
        name="decayed_scores",
    )(live_length, receptance, keys, log_decay)


def body(
    tokens, receptance, keys, log_decay, value_weight, noise_in, noise_out, utilities, live_length
):
    _, length, width = receptance.shape
    tokens, receptance, keys, log_decay = (
        a.reshape(length, width) for a in (tokens, receptance, keys, log_decay)
    )
    rows = value_weight.shape[0]
    wide = width // len(ROUTES)

    z = lax.axis_index("z")
    packed = pl.pallas_call(
        pack_kernel,
        out_shape=jax.ShapeDtypeStruct((rows + 8, width), BF16),
        in_specs=[SMEM] + [VMEM] * 3,
        out_specs=VMEM,
        name="weight_and_noise",
    )(utilities, value_weight, noise_in, noise_out)
    near = jnp.zeros((SIDE * rows, width), BF16)
    parts = []
    for step in (0, 1, 3, 2):
        parts.append(fetch(packed, "z", step) if step else packed)
        near = lax.dynamic_update_slice(
            near, parts[-1][:rows], (lax.rem(z + step, SIDE) * rows, 0)
        )
    mate = swap(tokens, "core", 1)
    scores = score_heads(live_length, receptance, keys, log_decay)
    near, mate, scores = lax.optimization_barrier((near, mate, scores))

    twin = swap(after(tokens, near), "twin", 1)

    chunks = range(len(ROUTES))
    held = [near[:, c * wide : (c + 1) * wide] for c in chunks]
    for step in range(2):
        came = [swap(held[c], *LINKS[ROUTES[c][step]]) for c in chunks]
        held = [jnp.concatenate([a, b], 0) for a, b in zip(held, came)]
    third = [swap(held[c], *LINKS[ROUTES[c][2]]) for c in chunks]
    parts = after(parts, *held)
    message = pl.pallas_call(
        message_kernel,
        out_shape=jax.ShapeDtypeStruct((SIDE * SIDE, SIDE, wide + width), F32),
        in_specs=[VMEM] * SIDE,
        out_specs=VMEM,
        compiler_params=params(60),
        cost_estimate=cost(0, 1 << 20),
        name="noise_message",
    )(*parts)
    held[0] = after(held[0], message)
    message = lax.all_to_all(message, ("y", "x"), split_axis=0, concat_axis=0, tiled=True)
    fourth = [swap(held[c], *LINKS[ROUTES[c][3]]) for c in chunks]

    both = swap(after(twin, *third), "core", 1)
    tp = lax.axis_index(TP).reshape(1)
    all_tokens, projected = pl.pallas_call(
        token_kernel,
        out_shape=[
            jax.ShapeDtypeStruct((4, length, width), BF16),
            jax.ShapeDtypeStruct((length, 8), F32),
        ],
        in_specs=[SMEM] + [VMEM] * 5,
        out_specs=[VMEM] * 2,
        cost_estimate=cost(0, 8 << 20),
        compiler_params=params(16),
        name="member_tokens",
    )(tp, tokens, mate, twin, both, noise_in.reshape(4, 1, width))

    update = pl.pallas_call(
        update_kernel,
        out_shape=jax.ShapeDtypeStruct((rows, width), F32),
        in_specs=[SMEM, VMEM],
        out_specs=VMEM,
        scratch_shapes=[pltpu.VMEM((SIDE**3, wide + width), F32)],
        compiler_params=params(8),
        cost_estimate=cost(0, 2 << 20),
        name="update_product",
    )(z.reshape(1), message)

    at = jnp.stack([lax.axis_index("y"), lax.axis_index("x")])
    ready = [after(third[0], message)] + third[1:]
    last = [swap(ready[c], *LINKS[ROUTES[c][3]]) for c in chunks]
    total = product(
        at, all_tokens, ((), (2,)), [p for c in chunks for p in (held[c], third[c])]
    )
    total = product(at, all_tokens, ((3,),), fourth, total)
    wkv_out = pl.pallas_call(
        readout_kernel,
        out_shape=jax.ShapeDtypeStruct((length, width), BF16),
        in_specs=[SMEM] + [VMEM] * 5 + [ANY] * len(last),
        out_specs=VMEM,
        scratch_shapes=[
            pltpu.VMEM((len(last),) + last[0].shape, BF16),
            pltpu.SemaphoreType.DMA((len(last),)),
        ],
        cost_estimate=cost(length * width * 2 * 1024, 12 << 20),
        compiler_params=params(20),
        name="values_readout",
    )(at, all_tokens, total, projected, noise_out, scores, *last)
    return wkv_out.reshape(1, length, width), update


def solution(mesh):
    mesh = Mesh(mesh.devices.reshape(SIDE, SIDE, SIDE, 2, 2), POP + TP)
    return jax.shard_map(
        body,
        mesh=mesh,
        in_specs=(
            P(POP, None, TP),
            P(POP, None, TP),
            P(POP, None, TP),
            P(POP, None, TP),
            P(POP, TP),
            P(POP, None),
            P(POP, TP),
            P(POP),
            P(POP),
        ),
        out_specs=(P(POP, None, TP), P(POP, TP)),
        check_vma=False,
    )
```

```python
import functools
import math

import jax
import jax.numpy as jnp
from jax import lax
from jax.experimental import pallas as pl
from jax.experimental.pallas import tpu as pltpu
from jax.sharding import Mesh, PartitionSpec as P

HEAD = 64
SIGMA = 0.5
HIGHEST = lax.Precision.HIGHEST
F32 = jnp.float32
BF16 = jnp.bfloat16

SIDE = 4
SPAN = 64
LANES = 128
POP = ("y", "x", "z")
TP = ("twin", "core")

LINKS = {"a": ("x", 1), "b": ("x", 3), "c": ("y", 1), "d": ("y", 3)}
ROUTES = ("acbd", "cadb", "bdac", "dbca")

ANY = pl.BlockSpec(memory_space=pl.ANY)
VMEM = pl.BlockSpec(memory_space=pltpu.VMEM)
SMEM = pl.BlockSpec(memory_space=pltpu.SMEM)


def swap(array, axis, mask):
    size = lax.axis_size(axis)
    return lax.ppermute(array, axis, [(i, i ^ mask) for i in range(size)])


def fetch(array, axis, step):
    size = lax.axis_size(axis)
    return lax.ppermute(array, axis, [((i + step) % size, i) for i in range(size)])


def masks(route, steps):
    found = []
    for i in range(4):
        y = x = 0
        for link in [route[k] for k in range(2) if (i >> k) & 1] + [route[k] for k in steps]:
            axis, mask = LINKS[link]
            y, x = (y ^ mask, x) if axis == "y" else (y, x ^ mask)
        found.append((y, x))
    return found


def token_kernel(at_ref, t0, t1, t2, t3, noise_ref, tokens_ref, projected_ref):
    total = None
    for bits, part in enumerate((t0, t1, t2, t3)):
        place = jnp.bitwise_xor(at_ref[0], bits)
        block = part[...]
        tokens_ref[place] = block
        noise = jnp.broadcast_to(noise_ref[place], (8, block.shape[1]))
        term = lax.dot_general(
            block, noise, (((1,), (1,)), ((), ())), preferred_element_type=F32
        )
        total = term if total is None else total + term
    projected_ref[...] = total


def halves(value):
    high = value.astype(BF16)
    return high, (value - high.astype(F32)).astype(BF16)


def score_kernel(live_ref, recept_ref, keys_ref, decay_ref, out_ref):
    length = recept_ref.shape[0]
    live = live_ref[0]
    row = lax.broadcasted_iota(jnp.int32, (length, LANES), 0)
    alive = row < live
    decay = jnp.where(alive, decay_ref[...], jnp.zeros((), BF16))
    keys = jnp.where(alive, keys_ref[...].astype(F32), 0.0)
    lower = (
        lax.broadcasted_iota(jnp.int32, (length, length), 0)
        >= lax.broadcasted_iota(jnp.int32, (length, length), 1)
    ).astype(F32).astype(BF16)
    summed = jnp.dot(lower, decay, preferred_element_type=F32)
    lane = lax.broadcasted_iota(jnp.int32, (SPAN, LANES), 1)
    across = (((1,), (1,)), ((), ()))
    for chunk in range(length // SPAN):
        first, last = chunk * SPAN, (chunk + 1) * SPAN
        base = summed[first - 1 : first] if chunk else jnp.zeros((1, LANES), F32)
        grown = recept_ref[first:last].astype(F32) * jnp.exp(summed[first:last] - base)
        shrunk_high, shrunk_low = halves(keys[:last] * jnp.exp(base - summed[:last]))
        both = jnp.concatenate(
            [jnp.where(lane < HEAD, grown, 0.0), jnp.where(lane < HEAD, 0.0, grown)], 0
        )
        both_high, both_low = halves(both)
        scores = lax.dot_general(
            jnp.concatenate([both_high, both_low], 0), shrunk_high, across, preferred_element_type=F32
        )
        scores = (
            scores[: 2 * SPAN]
            + scores[2 * SPAN :]
            + lax.dot_general(both_high, shrunk_low, across, preferred_element_type=F32)
        )
        here = lax.broadcasted_iota(jnp.int32, (SPAN, last), 0) + first
        there = lax.broadcasted_iota(jnp.int32, (SPAN, last), 1)
        kept = (here >= there) & (here < live)
        for head in range(2):
            parts = halves(jnp.where(kept, scores[head * SPAN : (head + 1) * SPAN], 0.0))
            for i, part in enumerate(parts):
                start = (2 * i + head) * length + first
                out_ref[0, start : start + SPAN, :last] = part
                if last < length:
                    out_ref[0, start : start + SPAN, last:] = jnp.zeros((SPAN, length - last), BF16)


def chunk_product(at_ref, tokens_ref, piece, blocks):
    depth = piece.shape[0] // len(blocks)
    columns = []
    for y, x in blocks:
        place = pl.multiple_of(jnp.bitwise_xor(at_ref[1], x) * depth, depth)
        columns.append(tokens_ref[jnp.bitwise_xor(at_ref[0], y), :, pl.ds(place, depth)])
    return jnp.dot(jnp.concatenate(columns, 1), piece[...], preferred_element_type=F32)


def copies_of(pieces, held, sems):
    copies = [pltpu.make_async_copy(p, held.at[i], sems.at[i]) for i, p in enumerate(pieces)]
    for copy in copies:
        copy.start()
    return copies


def product_kernel(ways, added, at_ref, tokens_ref, *refs):
    refs = list(refs)
    sum_ref = refs.pop(0) if added else None
    out_ref, held, sems = refs[-3:]
    wide = held.shape[2]
    copies = copies_of(refs[:-3], held, sems)
    for c, route in enumerate(ROUTES):
        where = slice(c * wide, (c + 1) * wide)
        total = sum_ref[:, where] if added else None
        for i, steps in enumerate(ways):
            at = c * len(ways) + i
            copies[at].wait()
            term = chunk_product(at_ref, tokens_ref, held.at[at], masks(route, steps))
            total = term if total is None else total + term
        out_ref[:, where] = total


def product(at, tokens, ways, pieces, before=None):
    length, width = tokens.shape[1:]
    extra = () if before is None else (before,)
    return pl.pallas_call(
        functools.partial(product_kernel, ways, before is not None),
        out_shape=jax.ShapeDtypeStruct((length, width), F32),
        in_specs=[SMEM, VMEM] + [VMEM] * len(extra) + [ANY] * len(pieces),
        out_specs=VMEM,
        scratch_shapes=[
            pltpu.VMEM((len(pieces),) + pieces[0].shape, BF16),
            pltpu.SemaphoreType.DMA((len(pieces),)),
        ],
        cost_estimate=cost(len(pieces) * 2 * length * pieces[0].size, 8 << 20),
        compiler_params=params(20),
        name="products",
    )(at, tokens, *extra, *pieces)


def readout_kernel(at_ref, tokens_ref, sum_ref, projected_ref, noise_ref, scores_ref, *refs):
    out_ref, held, sems = refs[-3:]
    wide = held.shape[2]
    copies = copies_of(refs[:-3], held, sems)
    projected = projected_ref[...][:, :1] * (
        SIGMA / math.sqrt(tokens_ref.shape[0] * tokens_ref.shape[2])
    )
    length = out_ref.shape[0]
    lane = lax.broadcasted_iota(jnp.int32, (length, LANES), 1)
    for c, route in enumerate(ROUTES):
        where = slice(c * wide, (c + 1) * wide)
        total = sum_ref[:, where] + projected * noise_ref[:, where].astype(F32)
        copies[c].wait()
        total = total + chunk_product(at_ref, tokens_ref, held.at[c], masks(route, (2, 3)))
        values = total.astype(BF16)
        for pair in range(wide // LANES):
            mine = values[:, pair * LANES : (pair + 1) * LANES]
            outs = jnp.dot(
                scores_ref[c * (wide // LANES) + pair], mine, preferred_element_type=F32
            )
            outs = outs[: 2 * length] + outs[2 * length :]
            start = c * wide + pair * LANES
            out_ref[:, start : start + LANES] = jnp.where(
                lane < HEAD, outs[:length], outs[length:]
            ).astype(BF16)


def message_kernel(utility_ref, noise_in_ref, noise_out_ref, out_ref):
    weighted = noise_in_ref[...].astype(F32) * (utility_ref[0] / math.sqrt(SIDE**3))
    plain = noise_out_ref[...].astype(F32)
    for i in range(out_ref.shape[0]):
        first = i // 2 * LANES
        out_ref[i, :, :LANES] = weighted[:, first : first + LANES]
        out_ref[i, :, LANES:] = plain


def update_kernel(z_ref, message_ref, out_ref):
    rows = out_ref.shape[0]
    message = message_ref[:, 0, :]
    weighted = pltpu.roll(message[:, :LANES], lax.rem(z_ref[0], 2) * rows, 1)
    out_ref[...] = lax.dot_general(
        weighted,
        message[:, LANES:],
        (((0,), (0,)), ((), ())),
        precision=HIGHEST,
        preferred_element_type=F32,
    )[:rows]


def params(mib):
    return pltpu.CompilerParams(vmem_limit_bytes=mib << 20)


def cost(flops, moved):
    return pl.CostEstimate(flops=flops, bytes_accessed=moved, transcendentals=0)


def after(value, *others):
    return lax.optimization_barrier((value, others))[0]


def score_heads(live_length, receptance, keys, log_decay):
    length, width = receptance.shape
    count = width // LANES
    strip = pl.BlockSpec((length, LANES), lambda i: (0, i))
    return pl.pallas_call(
        score_kernel,
        out_shape=jax.ShapeDtypeStruct((count, 4 * length, length), BF16),
        grid=(count,),
        in_specs=[SMEM, strip, strip, strip],
        out_specs=pl.BlockSpec((1, 4 * length, length), lambda i: (i, 0, 0)),
        cost_estimate=cost(0, 20 << 20),
        name="decayed_scores",
    )(live_length, receptance, keys, log_decay)


def body(
    tokens, receptance, keys, log_decay, value_weight, noise_in, noise_out, utilities, live_length
):
    _, length, width = receptance.shape
    tokens, receptance, keys, log_decay = (
        a.reshape(length, width) for a in (tokens, receptance, keys, log_decay)
    )
    rows = value_weight.shape[0]
    wide = width // len(ROUTES)

    z = lax.axis_index("z")
    near = jnp.zeros((SIDE * rows, width), BF16)
    for step in (0, 1, 3, 2):
        part = fetch(value_weight, "z", step) if step else value_weight
        near = lax.dynamic_update_slice(near, part, (lax.rem(z + step, SIDE) * rows, 0))
    mate = swap(tokens, "core", 1)
    population = lax.axis_size(POP)
    message = pl.pallas_call(
        message_kernel,
        out_shape=jax.ShapeDtypeStruct((population, 1, LANES + width), F32),
        in_specs=[SMEM, VMEM, VMEM],
        out_specs=VMEM,
        cost_estimate=cost(0, 1 << 19),
        name="noise_message",
    )(utilities, noise_in, noise_out)
    scores = score_heads(live_length, receptance, keys, log_decay)
    near, mate, message, scores = lax.optimization_barrier((near, mate, message, scores))

    twin = swap(after(tokens, near), "twin", 1)

    chunks = range(len(ROUTES))
    held = [near[:, c * wide : (c + 1) * wide] for c in chunks]
    for step in range(2):
        came = [swap(held[c], *LINKS[ROUTES[c][step]]) for c in chunks]
        held = [jnp.concatenate([a, b], 0) for a, b in zip(held, came)]
    message = lax.all_to_all(
        after(message, *held), POP, split_axis=0, concat_axis=0, tiled=True
    )
    third = [swap(held[c], *LINKS[ROUTES[c][2]]) for c in chunks]
    fourth = [swap(held[c], *LINKS[ROUTES[c][3]]) for c in chunks]
    ready = list(third)
    ready[3] = after(third[3], message)
    last = [swap(ready[c], *LINKS[ROUTES[c][3]]) for c in chunks]

    both = swap(after(twin, *third), "core", 1)
    tp = lax.axis_index(TP).reshape(1)
    all_tokens, projected = pl.pallas_call(
        token_kernel,
        out_shape=[
            jax.ShapeDtypeStruct((4, length, width), BF16),
            jax.ShapeDtypeStruct((length, 8), F32),
        ],
        in_specs=[SMEM] + [VMEM] * 5,
        out_specs=[VMEM] * 2,
        cost_estimate=cost(0, 8 << 20),
        compiler_params=params(16),
        name="member_tokens",
    )(tp, tokens, mate, twin, both, noise_in.reshape(4, 1, width))

    update = pl.pallas_call(
        update_kernel,
        out_shape=jax.ShapeDtypeStruct((rows, width), F32),
        in_specs=[SMEM, VMEM],
        out_specs=VMEM,
        cost_estimate=cost(0, 1 << 20),
        name="update_product",
    )(z.reshape(1), message)

    at = jnp.stack([lax.axis_index("y"), lax.axis_index("x")])
    total = product(
        at, all_tokens, ((), (2,)), [p for c in chunks for p in (held[c], third[c])]
    )
    total = product(at, all_tokens, ((3,),), fourth, total)
    wkv_out = pl.pallas_call(
        readout_kernel,
        out_shape=jax.ShapeDtypeStruct((length, width), BF16),
        in_specs=[SMEM] + [VMEM] * 5 + [ANY] * len(last),
        out_specs=VMEM,
        scratch_shapes=[
            pltpu.VMEM((len(last),) + last[0].shape, BF16),
            pltpu.SemaphoreType.DMA((len(last),)),
        ],
        cost_estimate=cost(length * width * 2 * 1024, 12 << 20),
        compiler_params=params(20),
        name="values_readout",
    )(at, all_tokens, total, projected, noise_out, scores, *last)
    return wkv_out.reshape(1, length, width), update


def solution(mesh):
    mesh = Mesh(mesh.devices.reshape(SIDE, SIDE, SIDE, 2, 2), POP + TP)
    return jax.shard_map(
        body,
        mesh=mesh,
        in_specs=(
            P(POP, None, TP),
            P(POP, None, TP),
            P(POP, None, TP),
            P(POP, None, TP),
            P(POP, TP),
            P(POP, None),
            P(POP, TP),
            P(POP),
            P(POP),
        ),
        out_specs=(P(POP, None, TP), P(POP, TP)),
        check_vma=False,
    )
```

```python
import functools
import math

import jax
import jax.numpy as jnp
from jax import lax
from jax.experimental import pallas as pl
from jax.experimental.pallas import tpu as pltpu
from jax.sharding import Mesh, PartitionSpec as P

HEAD = 64
SIGMA = 0.5
HIGHEST = lax.Precision.HIGHEST
F32 = jnp.float32
BF16 = jnp.bfloat16

SIDE = 4
SPAN = 64
LANES = 128
POP = ("y", "x", "z")
TP = ("twin", "core")

LINKS = {"a": ("x", 1), "b": ("x", 3), "c": ("y", 1), "d": ("y", 3)}
ROUTES = ("acbd", "cadb", "bdac", "dbca")

ANY = pl.BlockSpec(memory_space=pl.ANY)
VMEM = pl.BlockSpec(memory_space=pltpu.VMEM)
SMEM = pl.BlockSpec(memory_space=pltpu.SMEM)


def swap(array, axis, mask):
    size = lax.axis_size(axis)
    return lax.ppermute(array, axis, [(i, i ^ mask) for i in range(size)])


def fetch(array, axis, step):
    size = lax.axis_size(axis)
    return lax.ppermute(array, axis, [((i + step) % size, i) for i in range(size)])


def masks(route, steps):
    found = []
    for i in range(4):
        y = x = 0
        for link in [route[k] for k in range(2) if (i >> k) & 1] + [route[k] for k in steps]:
            axis, mask = LINKS[link]
            y, x = (y ^ mask, x) if axis == "y" else (y, x ^ mask)
        found.append((y, x))
    return found


def token_kernel(at_ref, t0, t1, t2, t3, noise_ref, tokens_ref, projected_ref):
    total = None
    for bits, part in enumerate((t0, t1, t2, t3)):
        place = jnp.bitwise_xor(at_ref[0], bits)
        block = part[...]
        tokens_ref[place] = block
        noise = jnp.broadcast_to(noise_ref[place], (8, block.shape[1]))
        term = lax.dot_general(
            block, noise, (((1,), (1,)), ((), ())), preferred_element_type=F32
        )
        total = term if total is None else total + term
    projected_ref[...] = total


def halves(value):
    high = value.astype(BF16)
    return high, (value - high.astype(F32)).astype(BF16)


def score_kernel(live_ref, recept_ref, keys_ref, decay_ref, out_ref):
    length = recept_ref.shape[0]
    live = live_ref[0]
    row = lax.broadcasted_iota(jnp.int32, (length, LANES), 0)
    alive = row < live
    decay = jnp.where(alive, decay_ref[...], jnp.zeros((), BF16))
    keys = jnp.where(alive, keys_ref[...].astype(F32), 0.0)
    lower = (
        lax.broadcasted_iota(jnp.int32, (length, length), 0)
        >= lax.broadcasted_iota(jnp.int32, (length, length), 1)
    ).astype(F32).astype(BF16)
    summed = jnp.dot(lower, decay, preferred_element_type=F32)
    lane = lax.broadcasted_iota(jnp.int32, (SPAN, LANES), 1)
    across = (((1,), (1,)), ((), ()))
    for chunk in range(length // SPAN):
        first, last = chunk * SPAN, (chunk + 1) * SPAN
        base = summed[first - 1 : first] if chunk else jnp.zeros((1, LANES), F32)
        grown = recept_ref[first:last].astype(F32) * jnp.exp(summed[first:last] - base)
        shrunk_high, shrunk_low = halves(keys[:last] * jnp.exp(base - summed[:last]))
        both = jnp.concatenate(
            [jnp.where(lane < HEAD, grown, 0.0), jnp.where(lane < HEAD, 0.0, grown)], 0
        )
        both_high, both_low = halves(both)
        scores = lax.dot_general(
            jnp.concatenate([both_high, both_low], 0), shrunk_high, across, preferred_element_type=F32
        )
        scores = (
            scores[: 2 * SPAN]
            + scores[2 * SPAN :]
            + lax.dot_general(both_high, shrunk_low, across, preferred_element_type=F32)
        )
        here = lax.broadcasted_iota(jnp.int32, (SPAN, last), 0) + first
        there = lax.broadcasted_iota(jnp.int32, (SPAN, last), 1)
        kept = (here >= there) & (here < live)
        for head in range(2):
            parts = halves(jnp.where(kept, scores[head * SPAN : (head + 1) * SPAN], 0.0))
            for i, part in enumerate(parts):
                start = (2 * i + head) * length + first
                out_ref[0, start : start + SPAN, :last] = part
                if last < length:
                    out_ref[0, start : start + SPAN, last:] = jnp.zeros((SPAN, length - last), BF16)


def chunk_product(at_ref, tokens_ref, piece, blocks):
    depth = piece.shape[0] // len(blocks)
    columns = []
    for y, x in blocks:
        place = pl.multiple_of(jnp.bitwise_xor(at_ref[1], x) * depth, depth)
        columns.append(tokens_ref[jnp.bitwise_xor(at_ref[0], y), :, pl.ds(place, depth)])
    return jnp.dot(jnp.concatenate(columns, 1), piece[...], preferred_element_type=F32)


def copies_of(pieces, held, sems):
    copies = [pltpu.make_async_copy(p, held.at[i], sems.at[i]) for i, p in enumerate(pieces)]
    for copy in copies:
        copy.start()
    return copies


def product_kernel(ways, added, at_ref, tokens_ref, *refs):
    refs = list(refs)
    sum_ref = refs.pop(0) if added else None
    out_ref, held, sems = refs[-3:]
    wide = held.shape[2]
    copies = copies_of(refs[:-3], held, sems)
    for c, route in enumerate(ROUTES):
        where = slice(c * wide, (c + 1) * wide)
        total = sum_ref[:, where] if added else None
        for i, steps in enumerate(ways):
            at = c * len(ways) + i
            copies[at].wait()
            term = chunk_product(at_ref, tokens_ref, held.at[at], masks(route, steps))
            total = term if total is None else total + term
        out_ref[:, where] = total


def product(at, tokens, ways, pieces, before=None):
    length, width = tokens.shape[1:]
    extra = () if before is None else (before,)
    return pl.pallas_call(
        functools.partial(product_kernel, ways, before is not None),
        out_shape=jax.ShapeDtypeStruct((length, width), F32),
        in_specs=[SMEM, VMEM] + [VMEM] * len(extra) + [ANY] * len(pieces),
        out_specs=VMEM,
        scratch_shapes=[
            pltpu.VMEM((len(pieces),) + pieces[0].shape, BF16),
            pltpu.SemaphoreType.DMA((len(pieces),)),
        ],
        cost_estimate=cost(len(pieces) * 2 * length * pieces[0].size, 8 << 20),
        compiler_params=params(20),
        name="products",
    )(at, tokens, *extra, *pieces)


def readout_kernel(at_ref, tokens_ref, sum_ref, projected_ref, noise_ref, scores_ref, *refs):
    out_ref, held, sems = refs[-3:]
    wide = held.shape[2]
    copies = copies_of(refs[:-3], held, sems)
    projected = projected_ref[...][:, :1] * (
        SIGMA / math.sqrt(tokens_ref.shape[0] * tokens_ref.shape[2])
    )
    length = out_ref.shape[0]
    lane = lax.broadcasted_iota(jnp.int32, (length, LANES), 1)
    for c, route in enumerate(ROUTES):
        where = slice(c * wide, (c + 1) * wide)
        total = sum_ref[:, where] + projected * noise_ref[:, where].astype(F32)
        copies[c].wait()
        total = total + chunk_product(at_ref, tokens_ref, held.at[c], masks(route, (2, 3)))
        values = total.astype(BF16)
        for pair in range(wide // LANES):
            mine = values[:, pair * LANES : (pair + 1) * LANES]
            outs = jnp.dot(
                scores_ref[c * (wide // LANES) + pair], mine, preferred_element_type=F32
            )
            outs = outs[: 2 * length] + outs[2 * length :]
            start = c * wide + pair * LANES
            out_ref[:, start : start + LANES] = jnp.where(
                lane < HEAD, outs[:length], outs[length:]
            ).astype(BF16)


def message_kernel(utility_ref, noise_in_ref, noise_out_ref, out_ref):
    weighted = noise_in_ref[...].astype(F32) * (utility_ref[0] / math.sqrt(SIDE**3))
    plain = noise_out_ref[...].astype(F32)
    for i in range(out_ref.shape[0]):
        first = i // 2 * LANES
        out_ref[i, :, :LANES] = weighted[:, first : first + LANES]
        out_ref[i, :, LANES:] = plain


def update_kernel(z_ref, message_ref, out_ref):
    rows = out_ref.shape[0]
    message = message_ref[:, 0, :]
    weighted = pltpu.roll(message[:, :LANES], lax.rem(z_ref[0], 2) * rows, 1)
    out_ref[...] = lax.dot_general(
        weighted,
        message[:, LANES:],
        (((0,), (0,)), ((), ())),
        precision=HIGHEST,
        preferred_element_type=F32,
    )[:rows]


def params(mib):
    return pltpu.CompilerParams(vmem_limit_bytes=mib << 20)


def cost(flops, moved):
    return pl.CostEstimate(flops=flops, bytes_accessed=moved, transcendentals=0)


def after(value, *others):
    return lax.optimization_barrier((value, others))[0]


def score_heads(live_length, receptance, keys, log_decay):
    length, width = receptance.shape
    count = width // LANES
    strip = pl.BlockSpec((length, LANES), lambda i: (0, i))
    return pl.pallas_call(
        score_kernel,
        out_shape=jax.ShapeDtypeStruct((count, 4 * length, length), BF16),
        grid=(count,),
        in_specs=[SMEM, strip, strip, strip],
        out_specs=pl.BlockSpec((1, 4 * length, length), lambda i: (i, 0, 0)),
        cost_estimate=cost(0, 20 << 20),
        name="decayed_scores",
    )(live_length, receptance, keys, log_decay)


def body(
    tokens, receptance, keys, log_decay, value_weight, noise_in, noise_out, utilities, live_length
):
    _, length, width = receptance.shape
    tokens, receptance, keys, log_decay = (
        a.reshape(length, width) for a in (tokens, receptance, keys, log_decay)
    )
    rows = value_weight.shape[0]
    wide = width // len(ROUTES)

    z = lax.axis_index("z")
    near = jnp.zeros((SIDE * rows, width), BF16)
    for step in (0, 1, 3, 2):
        part = fetch(value_weight, "z", step) if step else value_weight
        near = lax.dynamic_update_slice(near, part, (lax.rem(z + step, SIDE) * rows, 0))
    mate = swap(tokens, "core", 1)
    population = lax.axis_size(POP)
    message = pl.pallas_call(
        message_kernel,
        out_shape=jax.ShapeDtypeStruct((population, 1, LANES + width), F32),
        in_specs=[SMEM, VMEM, VMEM],
        out_specs=VMEM,
        cost_estimate=cost(0, 1 << 19),
        name="noise_message",
    )(utilities, noise_in, noise_out)
    scores = score_heads(live_length, receptance, keys, log_decay)
    near, mate, message, scores = lax.optimization_barrier((near, mate, message, scores))

    twin = swap(after(tokens, near), "twin", 1)

    chunks = range(len(ROUTES))
    held = [near[:, c * wide : (c + 1) * wide] for c in chunks]
    for step in range(2):
        came = [swap(held[c], *LINKS[ROUTES[c][step]]) for c in chunks]
        held = [jnp.concatenate([a, b], 0) for a, b in zip(held, came)]
    message = lax.all_to_all(
        after(message, *held), POP, split_axis=0, concat_axis=0, tiled=True
    )
    third = [swap(held[c], *LINKS[ROUTES[c][2]]) for c in chunks]
    fourth = [swap(held[c], *LINKS[ROUTES[c][3]]) for c in chunks]

    both = swap(after(twin, *third), "core", 1)
    tp = lax.axis_index(TP).reshape(1)
    all_tokens, projected = pl.pallas_call(
        token_kernel,
        out_shape=[
            jax.ShapeDtypeStruct((4, length, width), BF16),
            jax.ShapeDtypeStruct((length, 8), F32),
        ],
        in_specs=[SMEM] + [VMEM] * 5,
        out_specs=[VMEM] * 2,
        cost_estimate=cost(0, 8 << 20),
        compiler_params=params(60),
        name="member_tokens",
    )(tp, tokens, mate, twin, both, noise_in.reshape(4, 1, width))

    update = pl.pallas_call(
        update_kernel,
        out_shape=jax.ShapeDtypeStruct((rows, width), F32),
        in_specs=[SMEM, VMEM],
        out_specs=VMEM,
        cost_estimate=cost(0, 1 << 20),
        name="update_product",
    )(z.reshape(1), message)

    at = jnp.stack([lax.axis_index("y"), lax.axis_index("x")])
    total = product(
        at, all_tokens, ((), (2,)), [p for c in chunks for p in (held[c], third[c])]
    )
    ready = [after(t, total) for t in third[:2]] + third[2:]
    ready[3] = after(ready[3], message)
    last = [swap(ready[c], *LINKS[ROUTES[c][3]]) for c in chunks]
    total = product(at, all_tokens, ((3,),), fourth, total)
    wkv_out = pl.pallas_call(
        readout_kernel,
        out_shape=jax.ShapeDtypeStruct((length, width), BF16),
        in_specs=[SMEM] + [VMEM] * 5 + [ANY] * len(last),
        out_specs=VMEM,
        scratch_shapes=[
            pltpu.VMEM((len(last),) + last[0].shape, BF16),
            pltpu.SemaphoreType.DMA((len(last),)),
        ],
        cost_estimate=cost(length * width * 2 * 1024, 12 << 20),
        compiler_params=params(20),
        name="values_readout",
    )(at, all_tokens, total, projected, noise_out, scores, *last)
    return wkv_out.reshape(1, length, width), update


def solution(mesh):
    mesh = Mesh(mesh.devices.reshape(SIDE, SIDE, SIDE, 2, 2), POP + TP)
    return jax.shard_map(
        body,
        mesh=mesh,
        in_specs=(
            P(POP, None, TP),
            P(POP, None, TP),
            P(POP, None, TP),
            P(POP, None, TP),
            P(POP, TP),
            P(POP, None),
            P(POP, TP),
            P(POP),
            P(POP),
        ),
        out_specs=(P(POP, None, TP), P(POP, TP)),
        check_vma=False,
    )
```

```python
import functools
import math

import jax
import jax.numpy as jnp
from jax import lax
from jax.experimental import pallas as pl
from jax.experimental.pallas import tpu as pltpu
from jax.sharding import Mesh, PartitionSpec as P

HEAD = 64
SIGMA = 0.5
HIGHEST = lax.Precision.HIGHEST
F32 = jnp.float32
BF16 = jnp.bfloat16

SIDE = 4
SPAN = 64
LANES = 128
POP = ("y", "x", "z")
TP = ("twin", "core")

LINKS = {"a": ("x", 1), "b": ("x", 3), "c": ("y", 1), "d": ("y", 3)}
ROUTES = ("acbd", "cadb", "bdac", "dbca")

ANY = pl.BlockSpec(memory_space=pl.ANY)
VMEM = pl.BlockSpec(memory_space=pltpu.VMEM)
SMEM = pl.BlockSpec(memory_space=pltpu.SMEM)


def swap(array, axis, mask):
    size = lax.axis_size(axis)
    return lax.ppermute(array, axis, [(i, i ^ mask) for i in range(size)])


def fetch(array, axis, step):
    size = lax.axis_size(axis)
    return lax.ppermute(array, axis, [((i + step) % size, i) for i in range(size)])


def masks(route, steps):
    found = []
    for i in range(4):
        y = x = 0
        for link in [route[k] for k in range(2) if (i >> k) & 1] + [route[k] for k in steps]:
            axis, mask = LINKS[link]
            y, x = (y ^ mask, x) if axis == "y" else (y, x ^ mask)
        found.append((y, x))
    return found


def token_kernel(at_ref, t0, t1, t2, t3, noise_ref, tokens_ref, projected_ref):
    total = None
    for bits, part in enumerate((t0, t1, t2, t3)):
        place = jnp.bitwise_xor(at_ref[0], bits)
        block = part[...]
        tokens_ref[place] = block
        noise = jnp.broadcast_to(noise_ref[place], (8, block.shape[1]))
        term = lax.dot_general(
            block, noise, (((1,), (1,)), ((), ())), preferred_element_type=F32
        )
        total = term if total is None else total + term
    projected_ref[...] = total


def halves(value):
    high = value.astype(BF16)
    return high, (value - high.astype(F32)).astype(BF16)


def score_kernel(live_ref, recept_ref, keys_ref, decay_ref, out_ref):
    length = recept_ref.shape[0]
    live = live_ref[0]
    row = lax.broadcasted_iota(jnp.int32, (length, LANES), 0)
    alive = row < live
    decay = jnp.where(alive, decay_ref[...], jnp.zeros((), BF16))
    keys = jnp.where(alive, keys_ref[...].astype(F32), 0.0)
    lower = (
        lax.broadcasted_iota(jnp.int32, (length, length), 0)
        >= lax.broadcasted_iota(jnp.int32, (length, length), 1)
    ).astype(F32).astype(BF16)
    summed = jnp.dot(lower, decay, preferred_element_type=F32)
    lane = lax.broadcasted_iota(jnp.int32, (SPAN, LANES), 1)
    across = (((1,), (1,)), ((), ()))
    for chunk in range(length // SPAN):
        first, last = chunk * SPAN, (chunk + 1) * SPAN
        base = summed[first - 1 : first] if chunk else jnp.zeros((1, LANES), F32)
        grown = recept_ref[first:last].astype(F32) * jnp.exp(summed[first:last] - base)
        shrunk_high, shrunk_low = halves(keys[:last] * jnp.exp(base - summed[:last]))
        both = jnp.concatenate(
            [jnp.where(lane < HEAD, grown, 0.0), jnp.where(lane < HEAD, 0.0, grown)], 0
        )
        both_high, both_low = halves(both)
        scores = lax.dot_general(
            jnp.concatenate([both_high, both_low], 0), shrunk_high, across, preferred_element_type=F32
        )
        scores = (
            scores[: 2 * SPAN]
            + scores[2 * SPAN :]
            + lax.dot_general(both_high, shrunk_low, across, preferred_element_type=F32)
        )
        here = lax.broadcasted_iota(jnp.int32, (SPAN, last), 0) + first
        there = lax.broadcasted_iota(jnp.int32, (SPAN, last), 1)
        kept = (here >= there) & (here < live)
        for head in range(2):
            parts = halves(jnp.where(kept, scores[head * SPAN : (head + 1) * SPAN], 0.0))
            for i, part in enumerate(parts):
                start = (2 * i + head) * length + first
                out_ref[0, start : start + SPAN, :last] = part
                if last < length:
                    out_ref[0, start : start + SPAN, last:] = jnp.zeros((SPAN, length - last), BF16)


def chunk_product(at_ref, tokens_ref, piece, blocks):
    depth = piece.shape[0] // len(blocks)
    columns = []
    for y, x in blocks:
        place = pl.multiple_of(jnp.bitwise_xor(at_ref[1], x) * depth, depth)
        columns.append(tokens_ref[jnp.bitwise_xor(at_ref[0], y), :, pl.ds(place, depth)])
    return jnp.dot(jnp.concatenate(columns, 1), piece[...], preferred_element_type=F32)


def copies_of(pieces, held, sems):
    copies = [pltpu.make_async_copy(p, held.at[i], sems.at[i]) for i, p in enumerate(pieces)]
    for copy in copies:
        copy.start()
    return copies


def product_kernel(ways, added, at_ref, tokens_ref, *refs):
    refs = list(refs)
    sum_ref = refs.pop(0) if added else None
    out_ref, held, sems = refs[-3:]
    wide = held.shape[2]
    copies = copies_of(refs[:-3], held, sems)
    for c, route in enumerate(ROUTES):
        where = slice(c * wide, (c + 1) * wide)
        total = sum_ref[:, where] if added else None
        for i, steps in enumerate(ways):
            at = c * len(ways) + i
            copies[at].wait()
            term = chunk_product(at_ref, tokens_ref, held.at[at], masks(route, steps))
            total = term if total is None else total + term
        out_ref[:, where] = total


def product(at, tokens, ways, pieces, before=None):
    length, width = tokens.shape[1:]
    extra = () if before is None else (before,)
    return pl.pallas_call(
        functools.partial(product_kernel, ways, before is not None),
        out_shape=jax.ShapeDtypeStruct((length, width), F32),
        in_specs=[SMEM, VMEM] + [VMEM] * len(extra) + [ANY] * len(pieces),
        out_specs=VMEM,
        scratch_shapes=[
            pltpu.VMEM((len(pieces),) + pieces[0].shape, BF16),
            pltpu.SemaphoreType.DMA((len(pieces),)),
        ],
        cost_estimate=cost(len(pieces) * 2 * length * pieces[0].size, 8 << 20),
        compiler_params=params(20),
        name="products",
    )(at, tokens, *extra, *pieces)


def readout_kernel(at_ref, tokens_ref, sum_ref, projected_ref, noise_ref, scores_ref, *refs):
    out_ref, held, sems = refs[-3:]
    wide = held.shape[2]
    copies = copies_of(refs[:-3], held, sems)
    projected = projected_ref[...][:, :1] * (
        SIGMA / math.sqrt(tokens_ref.shape[0] * tokens_ref.shape[2])
    )
    length = out_ref.shape[0]
    lane = lax.broadcasted_iota(jnp.int32, (length, LANES), 1)
    for c, route in enumerate(ROUTES):
        where = slice(c * wide, (c + 1) * wide)
        total = sum_ref[:, where] + projected * noise_ref[:, where].astype(F32)
        copies[c].wait()
        total = total + chunk_product(at_ref, tokens_ref, held.at[c], masks(route, (2, 3)))
        values = total.astype(BF16)
        for pair in range(wide // LANES):
            mine = values[:, pair * LANES : (pair + 1) * LANES]
            outs = jnp.dot(
                scores_ref[c * (wide // LANES) + pair], mine, preferred_element_type=F32
            )
            outs = outs[: 2 * length] + outs[2 * length :]
            start = c * wide + pair * LANES
            out_ref[:, start : start + LANES] = jnp.where(
                lane < HEAD, outs[:length], outs[length:]
            ).astype(BF16)


def message_kernel(utility_ref, noise_in_ref, noise_out_ref, out_ref):
    weighted = noise_in_ref[...].astype(F32) * (utility_ref[0] / math.sqrt(SIDE**3))
    plain = noise_out_ref[...].astype(F32)
    for i in range(out_ref.shape[0]):
        first = i // 2 * LANES
        out_ref[i, :, :LANES] = weighted[:, first : first + LANES]
        out_ref[i, :, LANES:] = plain


def update_kernel(z_ref, message_ref, out_ref):
    rows = out_ref.shape[0]
    message = message_ref[:, 0, :]
    weighted = pltpu.roll(message[:, :LANES], lax.rem(z_ref[0], 2) * rows, 1)
    out_ref[...] = lax.dot_general(
        weighted,
        message[:, LANES:],
        (((0,), (0,)), ((), ())),
        precision=HIGHEST,
        preferred_element_type=F32,
    )[:rows]


def params(mib):
    return pltpu.CompilerParams(vmem_limit_bytes=mib << 20)


def cost(flops, moved):
    return pl.CostEstimate(flops=flops, bytes_accessed=moved, transcendentals=0)


def after(value, *others):
    return lax.optimization_barrier((value, others))[0]


def score_heads(live_length, receptance, keys, log_decay):
    length, width = receptance.shape
    count = width // LANES
    strip = pl.BlockSpec((length, LANES), lambda i: (0, i))
    return pl.pallas_call(
        score_kernel,
        out_shape=jax.ShapeDtypeStruct((count, 4 * length, length), BF16),
        grid=(count,),
        in_specs=[SMEM, strip, strip, strip],
        out_specs=pl.BlockSpec((1, 4 * length, length), lambda i: (i, 0, 0)),
        cost_estimate=cost(0, 20 << 20),
        name="decayed_scores",
    )(live_length, receptance, keys, log_decay)


def body(
    tokens, receptance, keys, log_decay, value_weight, noise_in, noise_out, utilities, live_length
):
    _, length, width = receptance.shape
    tokens, receptance, keys, log_decay = (
        a.reshape(length, width) for a in (tokens, receptance, keys, log_decay)
    )
    rows = value_weight.shape[0]
    wide = width // len(ROUTES)

    z = lax.axis_index("z")
    near = jnp.zeros((SIDE * rows, width), BF16)
    for step in (0, 1, 3, 2):
        part = fetch(value_weight, "z", step) if step else value_weight
        near = lax.dynamic_update_slice(near, part, (lax.rem(z + step, SIDE) * rows, 0))
    mate = swap(tokens, "core", 1)
    population = lax.axis_size(POP)
    message = pl.pallas_call(
        message_kernel,
        out_shape=jax.ShapeDtypeStruct((population, 1, LANES + width), F32),
        in_specs=[SMEM, VMEM, VMEM],
        out_specs=VMEM,
        cost_estimate=cost(0, 1 << 19),
        name="noise_message",
    )(utilities, noise_in, noise_out)
    scores = score_heads(live_length, receptance, keys, log_decay)
    near, mate, message, scores = lax.optimization_barrier((near, mate, message, scores))

    twin = swap(after(tokens, near), "twin", 1)

    chunks = range(len(ROUTES))
    held = [near[:, c * wide : (c + 1) * wide] for c in chunks]
    for step in range(2):
        came = [swap(held[c], *LINKS[ROUTES[c][step]]) for c in chunks]
        held = [jnp.concatenate([a, b], 0) for a, b in zip(held, came)]
    message = lax.all_to_all(
        after(message, *held), POP, split_axis=0, concat_axis=0, tiled=True
    )
    third = [swap(held[c], *LINKS[ROUTES[c][2]]) for c in chunks]
    fourth = [swap(held[c], *LINKS[ROUTES[c][3]]) for c in chunks]
    update = pl.pallas_call(
        update_kernel,
        out_shape=jax.ShapeDtypeStruct((rows, width), F32),
        in_specs=[SMEM, VMEM],
        out_specs=VMEM,
        cost_estimate=cost(0, 1 << 20),
        name="update_product",
    )(z.reshape(1), message)

    ready = list(third)
    ready[3] = after(third[3], update)
    last = [swap(ready[c], *LINKS[ROUTES[c][3]]) for c in chunks]

    both = swap(after(twin, *third), "core", 1)
    tp = lax.axis_index(TP).reshape(1)
    all_tokens, projected = pl.pallas_call(
        token_kernel,
        out_shape=[
            jax.ShapeDtypeStruct((4, length, width), BF16),
            jax.ShapeDtypeStruct((length, 8), F32),
        ],
        in_specs=[SMEM] + [VMEM] * 5,
        out_specs=[VMEM] * 2,
        cost_estimate=cost(0, 8 << 20),
        compiler_params=params(16),
        name="member_tokens",
    )(tp, tokens, mate, twin, both, noise_in.reshape(4, 1, width))

    at = jnp.stack([lax.axis_index("y"), lax.axis_index("x")])
    total = product(
        at, all_tokens, ((), (2,)), [p for c in chunks for p in (held[c], third[c])]
    )
    total = product(at, all_tokens, ((3,),), fourth, total)
    wkv_out = pl.pallas_call(
        readout_kernel,
        out_shape=jax.ShapeDtypeStruct((length, width), BF16),
        in_specs=[SMEM] + [VMEM] * 5 + [ANY] * len(last),
        out_specs=VMEM,
        scratch_shapes=[
            pltpu.VMEM((len(last),) + last[0].shape, BF16),
            pltpu.SemaphoreType.DMA((len(last),)),
        ],
        cost_estimate=cost(length * width * 2 * 1024, 12 << 20),
        compiler_params=params(20),
        name="values_readout",
    )(at, all_tokens, total, projected, noise_out, scores, *last)
    return wkv_out.reshape(1, length, width), update


def solution(mesh):
    mesh = Mesh(mesh.devices.reshape(SIDE, SIDE, SIDE, 2, 2), POP + TP)
    return jax.shard_map(
        body,
        mesh=mesh,
        in_specs=(
            P(POP, None, TP),
            P(POP, None, TP),
            P(POP, None, TP),
            P(POP, None, TP),
            P(POP, TP),
            P(POP, None),
            P(POP, TP),
            P(POP),
            P(POP),
        ),
        out_specs=(P(POP, None, TP), P(POP, TP)),
        check_vma=False,
    )
```

```python
import functools
import math

import jax
import jax.numpy as jnp
from jax import lax
from jax.experimental import pallas as pl
from jax.experimental.pallas import tpu as pltpu
from jax.sharding import Mesh, PartitionSpec as P

HEAD = 64
SIGMA = 0.5
HIGHEST = lax.Precision.HIGHEST
F32 = jnp.float32
BF16 = jnp.bfloat16

SIDE = 4
SPAN = 64
LANES = 128
POP = ("y", "x", "z")
TP = ("twin", "core")

LINKS = {"a": ("x", 1), "b": ("x", 3), "c": ("y", 1), "d": ("y", 3)}
ROUTES = ("acbd", "cadb", "bdac", "dbca")

ANY = pl.BlockSpec(memory_space=pl.ANY)
VMEM = pl.BlockSpec(memory_space=pltpu.VMEM)
SMEM = pl.BlockSpec(memory_space=pltpu.SMEM)


def swap(array, axis, mask):
    size = lax.axis_size(axis)
    return lax.ppermute(array, axis, [(i, i ^ mask) for i in range(size)])


def fetch(array, axis, step):
    size = lax.axis_size(axis)
    return lax.ppermute(array, axis, [((i + step) % size, i) for i in range(size)])


def masks(route, steps):
    found = []
    for i in range(4):
        y = x = 0
        for link in [route[k] for k in range(2) if (i >> k) & 1] + [route[k] for k in steps]:
            axis, mask = LINKS[link]
            y, x = (y ^ mask, x) if axis == "y" else (y, x ^ mask)
        found.append((y, x))
    return found


def token_kernel(at_ref, t0, t1, t2, t3, noise_ref, tokens_ref, projected_ref):
    total = None
    for bits, part in enumerate((t0, t1, t2, t3)):
        place = jnp.bitwise_xor(at_ref[0], bits)
        block = part[...]
        tokens_ref[place] = block
        noise = jnp.broadcast_to(noise_ref[place], (8, block.shape[1]))
        term = lax.dot_general(
            block, noise, (((1,), (1,)), ((), ())), preferred_element_type=F32
        )
        total = term if total is None else total + term
    projected_ref[...] = total


def halves(value):
    high = value.astype(BF16)
    return high, (value - high.astype(F32)).astype(BF16)


def score_kernel(live_ref, recept_ref, keys_ref, decay_ref, out_ref):
    length = recept_ref.shape[0]
    live = live_ref[0]
    row = lax.broadcasted_iota(jnp.int32, (length, LANES), 0)
    alive = row < live
    decay = jnp.where(alive, decay_ref[...], jnp.zeros((), BF16))
    keys = jnp.where(alive, keys_ref[...].astype(F32), 0.0)
    lower = (
        lax.broadcasted_iota(jnp.int32, (length, length), 0)
        >= lax.broadcasted_iota(jnp.int32, (length, length), 1)
    ).astype(F32).astype(BF16)
    summed = jnp.dot(lower, decay, preferred_element_type=F32)
    lane = lax.broadcasted_iota(jnp.int32, (SPAN, LANES), 1)
    across = (((1,), (1,)), ((), ()))
    for chunk in range(length // SPAN):
        first, last = chunk * SPAN, (chunk + 1) * SPAN
        base = summed[first - 1 : first] if chunk else jnp.zeros((1, LANES), F32)
        grown = recept_ref[first:last].astype(F32) * jnp.exp(summed[first:last] - base)
        shrunk_high, shrunk_low = halves(keys[:last] * jnp.exp(base - summed[:last]))
        both = jnp.concatenate(
            [jnp.where(lane < HEAD, grown, 0.0), jnp.where(lane < HEAD, 0.0, grown)], 0
        )
        both_high, both_low = halves(both)
        scores = lax.dot_general(
            jnp.concatenate([both_high, both_low], 0), shrunk_high, across, preferred_element_type=F32
        )
        scores = (
            scores[: 2 * SPAN]
            + scores[2 * SPAN :]
            + lax.dot_general(both_high, shrunk_low, across, preferred_element_type=F32)
        )
        here = lax.broadcasted_iota(jnp.int32, (SPAN, last), 0) + first
        there = lax.broadcasted_iota(jnp.int32, (SPAN, last), 1)
        kept = (here >= there) & (here < live)
        for head in range(2):
            start = head * length + first
            mine = jnp.where(kept, scores[head * SPAN : (head + 1) * SPAN], 0.0)
            out_ref[0, start : start + SPAN, :last] = mine.astype(BF16)
            if last < length:
                out_ref[0, start : start + SPAN, last:] = jnp.zeros((SPAN, length - last), BF16)


def chunk_product(at_ref, tokens_ref, piece, blocks):
    depth = piece.shape[0] // len(blocks)
    columns = []
    for y, x in blocks:
        place = pl.multiple_of(jnp.bitwise_xor(at_ref[1], x) * depth, depth)
        columns.append(tokens_ref[jnp.bitwise_xor(at_ref[0], y), :, pl.ds(place, depth)])
    return jnp.dot(jnp.concatenate(columns, 1), piece[...], preferred_element_type=F32)


def copies_of(pieces, held, sems):
    copies = [pltpu.make_async_copy(p, held.at[i], sems.at[i]) for i, p in enumerate(pieces)]
    for copy in copies:
        copy.start()
    return copies


def product_kernel(ways, added, at_ref, tokens_ref, *refs):
    refs = list(refs)
    sum_ref = refs.pop(0) if added else None
    out_ref, held, sems = refs[-3:]
    wide = held.shape[2]
    copies = copies_of(refs[:-3], held, sems)
    for c, route in enumerate(ROUTES):
        where = slice(c * wide, (c + 1) * wide)
        total = sum_ref[:, where] if added else None
        for i, steps in enumerate(ways):
            at = c * len(ways) + i
            copies[at].wait()
            term = chunk_product(at_ref, tokens_ref, held.at[at], masks(route, steps))
            total = term if total is None else total + term
        out_ref[:, where] = total


def product(at, tokens, ways, pieces, before=None):
    length, width = tokens.shape[1:]
    extra = () if before is None else (before,)
    return pl.pallas_call(
        functools.partial(product_kernel, ways, before is not None),
        out_shape=jax.ShapeDtypeStruct((length, width), F32),
        in_specs=[SMEM, VMEM] + [VMEM] * len(extra) + [ANY] * len(pieces),
        out_specs=VMEM,
        scratch_shapes=[
            pltpu.VMEM((len(pieces),) + pieces[0].shape, BF16),
            pltpu.SemaphoreType.DMA((len(pieces),)),
        ],
        cost_estimate=cost(len(pieces) * 2 * length * pieces[0].size, 8 << 20),
        compiler_params=params(20),
        name="products",
    )(at, tokens, *extra, *pieces)


def readout_kernel(at_ref, tokens_ref, sum_ref, projected_ref, noise_ref, scores_ref, *refs):
    out_ref, held, sems = refs[-3:]
    wide = held.shape[2]
    copies = copies_of(refs[:-3], held, sems)
    projected = projected_ref[...][:, :1] * (
        SIGMA / math.sqrt(tokens_ref.shape[0] * tokens_ref.shape[2])
    )
    length = out_ref.shape[0]
    lane = lax.broadcasted_iota(jnp.int32, (length, LANES), 1)
    for c, route in enumerate(ROUTES):
        where = slice(c * wide, (c + 1) * wide)
        total = sum_ref[:, where] + projected * noise_ref[:, where].astype(F32)
        copies[c].wait()
        total = total + chunk_product(at_ref, tokens_ref, held.at[c], masks(route, (2, 3)))
        values = total.astype(BF16)
        for pair in range(wide // LANES):
            mine = values[:, pair * LANES : (pair + 1) * LANES]
            outs = jnp.dot(
                scores_ref[c * (wide // LANES) + pair], mine, preferred_element_type=F32
            )
            start = c * wide + pair * LANES
            out_ref[:, start : start + LANES] = jnp.where(
                lane < HEAD, outs[:length], outs[length:]
            ).astype(BF16)


def message_kernel(utility_ref, noise_in_ref, noise_out_ref, out_ref):
    weighted = noise_in_ref[...].astype(F32) * (utility_ref[0] / math.sqrt(SIDE**3))
    plain = noise_out_ref[...].astype(F32)
    for i in range(out_ref.shape[0]):
        first = i // 2 * LANES
        out_ref[i, :, :LANES] = weighted[:, first : first + LANES]
        out_ref[i, :, LANES:] = plain


def update_kernel(z_ref, message_ref, out_ref):
    rows = out_ref.shape[0]
    message = message_ref[:, 0, :]
    weighted = pltpu.roll(message[:, :LANES], lax.rem(z_ref[0], 2) * rows, 1)
    out_ref[...] = lax.dot_general(
        weighted,
        message[:, LANES:],
        (((0,), (0,)), ((), ())),
        precision=HIGHEST,
        preferred_element_type=F32,
    )[:rows]


def params(mib):
    return pltpu.CompilerParams(vmem_limit_bytes=mib << 20)


def cost(flops, moved):
    return pl.CostEstimate(flops=flops, bytes_accessed=moved, transcendentals=0)


def after(value, *others):
    return lax.optimization_barrier((value, others))[0]


def score_heads(live_length, receptance, keys, log_decay):
    length, width = receptance.shape
    count = width // LANES
    strip = pl.BlockSpec((length, LANES), lambda i: (0, i))
    return pl.pallas_call(
        score_kernel,
        out_shape=jax.ShapeDtypeStruct((count, 2 * length, length), BF16),
        grid=(count,),
        in_specs=[SMEM, strip, strip, strip],
        out_specs=pl.BlockSpec((1, 2 * length, length), lambda i: (i, 0, 0)),
        cost_estimate=cost(0, 20 << 20),
        name="decayed_scores",
    )(live_length, receptance, keys, log_decay)


def body(
    tokens, receptance, keys, log_decay, value_weight, noise_in, noise_out, utilities, live_length
):
    _, length, width = receptance.shape
    tokens, receptance, keys, log_decay = (
        a.reshape(length, width) for a in (tokens, receptance, keys, log_decay)
    )
    rows = value_weight.shape[0]
    wide = width // len(ROUTES)

    z = lax.axis_index("z")
    near = jnp.zeros((SIDE * rows, width), BF16)
    for step in (0, 1, 3, 2):
        part = fetch(value_weight, "z", step) if step else value_weight
        near = lax.dynamic_update_slice(near, part, (lax.rem(z + step, SIDE) * rows, 0))
    mate = swap(tokens, "core", 1)
    population = lax.axis_size(POP)
    message = pl.pallas_call(
        message_kernel,
        out_shape=jax.ShapeDtypeStruct((population, 1, LANES + width), F32),
        in_specs=[SMEM, VMEM, VMEM],
        out_specs=VMEM,
        cost_estimate=cost(0, 1 << 19),
        name="noise_message",
    )(utilities, noise_in, noise_out)
    scores = score_heads(live_length, receptance, keys, log_decay)
    near, mate, message, scores = lax.optimization_barrier((near, mate, message, scores))

    twin = swap(after(tokens, near), "twin", 1)

    chunks = range(len(ROUTES))
    held = [near[:, c * wide : (c + 1) * wide] for c in chunks]
    for step in range(2):
        came = [swap(held[c], *LINKS[ROUTES[c][step]]) for c in chunks]
        held = [jnp.concatenate([a, b], 0) for a, b in zip(held, came)]
    message = lax.all_to_all(
        after(message, *held), POP, split_axis=0, concat_axis=0, tiled=True
    )
    third = [swap(held[c], *LINKS[ROUTES[c][2]]) for c in chunks]
    fourth = [swap(held[c], *LINKS[ROUTES[c][3]]) for c in chunks]
    update = pl.pallas_call(
        update_kernel,
        out_shape=jax.ShapeDtypeStruct((rows, width), F32),
        in_specs=[SMEM, VMEM],
        out_specs=VMEM,
        cost_estimate=cost(0, 1 << 20),
        name="update_product",
    )(z.reshape(1), message)

    ready = list(third)
    ready[3] = after(third[3], update)
    last = [swap(ready[c], *LINKS[ROUTES[c][3]]) for c in chunks]

    both = swap(after(twin, *third), "core", 1)
    tp = lax.axis_index(TP).reshape(1)
    all_tokens, projected = pl.pallas_call(
        token_kernel,
        out_shape=[
            jax.ShapeDtypeStruct((4, length, width), BF16),
            jax.ShapeDtypeStruct((length, 8), F32),
        ],
        in_specs=[SMEM] + [VMEM] * 5,
        out_specs=[VMEM] * 2,
        cost_estimate=cost(0, 8 << 20),
        compiler_params=params(16),
        name="member_tokens",
    )(tp, tokens, mate, twin, both, noise_in.reshape(4, 1, width))

    at = jnp.stack([lax.axis_index("y"), lax.axis_index("x")])
    total = product(
        at, all_tokens, ((), (2,)), [p for c in chunks for p in (held[c], third[c])]
    )
    total = product(at, all_tokens, ((3,),), fourth, total)
    wkv_out = pl.pallas_call(
        readout_kernel,
        out_shape=jax.ShapeDtypeStruct((length, width), BF16),
        in_specs=[SMEM] + [VMEM] * 5 + [ANY] * len(last),
        out_specs=VMEM,
        scratch_shapes=[
            pltpu.VMEM((len(last),) + last[0].shape, BF16),
            pltpu.SemaphoreType.DMA((len(last),)),
        ],
        cost_estimate=cost(length * width * 2 * 1024, 12 << 20),
        compiler_params=params(20),
        name="values_readout",
    )(at, all_tokens, total, projected, noise_out, scores, *last)
    return wkv_out.reshape(1, length, width), update


def solution(mesh):
    mesh = Mesh(mesh.devices.reshape(SIDE, SIDE, SIDE, 2, 2), POP + TP)
    return jax.shard_map(
        body,
        mesh=mesh,
        in_specs=(
            P(POP, None, TP),
            P(POP, None, TP),
            P(POP, None, TP),
            P(POP, None, TP),
            P(POP, TP),
            P(POP, None),
            P(POP, TP),
            P(POP),
            P(POP),
        ),
        out_specs=(P(POP, None, TP), P(POP, TP)),
        check_vma=False,
    )
```
